512 devices in a mesh: rng: 32 (over y, x), xr: 16 (over z, core).
Axes of the slice: x: 4, y: 8, z: 8, core: 2. Of those that a mesh axis runs over, the one named last changes fastest.
Arguments:
- incident: float32 [4, 512, 2048], P(None, 'rng', 'xr'), may hold values from -6 to 6
- inverse_diag: float32 [4, 512, 2048], P(None, 'rng', 'xr'), may hold values from -4 to 4
- previous: float32 [4, 512, 2048], P(None, 'rng', 'xr'), may hold values from -4 to 4
- heights: float32 [512, 2048], P('rng', 'xr'), may hold values from -3 to 3
- neighbours: int32 [24, 512, 2048], P(None, 'rng', 'xr'), may hold values from 0 to 47, as said below
- counts: int32 [512, 2048], P('rng', 'xr'), may hold values from 1 to 24
- transmit: float32 [32, 2, 64], P('rng'), may hold values from 0.02 to 1
- angle_weights: float32 [2, 2, 64], replicated, may hold values from -0.15 to 0.15
Outputs:
- forward_currents: float32 [4, 512, 2048], P(None, 'rng', 'xr')
- currents: float32 [4, 512, 2048], P(None, 'rng', 'xr')
The draws below stay inside these ranges and needn't reach their ends.
Inputs may be any that keep to these rules, and one draw needn't show every extreme that they name: `neighbours`: the entries of one patch's list are distinct; slots at or beyond the patch's count hold entries that are not used.
All inputs are finite; a program needn't handle non-finite values.
Results may differ from the reference program's by a relative error of at most 0.0003.
Values sent between devices are 32-bit elements; how exact they have to be, the bound alone decides.
A program may use at most 128 MiB of HBM per device.

```python
import math
import jax
import jax.numpy as jnp
from jax import lax

F = 2
Q = 64
H = 3
LMAX = 24
RD = 16
XD = 128
OFFSETS = 48
RANGE_BLOCKS = 32
NR = 512
NC = 2048


def neighbour_tables(key):
    key = jax.random.fold_in(key, 311)
    score_key, steep_key, count_key = jax.random.split(key, 3)
    scores = jax.random.randint(score_key, (NR, NC, OFFSETS), 0, 2 ** 20) * 64 + jnp.arange(OFFSETS, dtype=jnp.int32)
    scores = scores.at[0, 0, OFFSETS - 1].set(2 ** 26 + 1).at[0, 0, 0].set(2 ** 26)
    _, picked = lax.top_k(scores, LMAX)
    offset_codes = jnp.moveaxis(picked, 2, 0)
    steep_blocks = jax.random.randint(steep_key, (NR // RD, NC // XD), 0, 8) == 0
    steep_blocks = steep_blocks.at[0, 0].set(True)
    cap_blocks = jnp.where(steep_blocks, LMAX, LMAX // 4)
    cap_cells = jnp.repeat(jnp.repeat(cap_blocks, RD, axis=0), XD, axis=1)
    slot_counts = jax.random.randint(count_key, (NR, NC), 1, cap_cells + 1).at[0, 0].set(LMAX)
    return (offset_codes.astype(jnp.int32), slot_counts.astype(jnp.int32))


def draw_neighbours(key, part):
    return neighbour_tables(key)[0]


def draw_counts(key, part):
    return neighbour_tables(key)[1]


def draw_heights(key, part):
    key = jax.random.fold_in(key, 701)
    level_key = jax.random.fold_in(key, 1)
    terrain = jax.random.uniform(level_key, (NR, NC), minval=-3.0, maxval=3.0)
    return terrain.astype(jnp.float32)


def draw_transmit(key, part):
    key = jax.random.fold_in(key, 523)
    selection_key, gradual_random_key, quick_random_key, spike_random_key, depth_random_key = jax.random.split(key, 5)
    slow_share = 0.5
    lasting = jax.random.uniform(selection_key, (1, F, Q)) < slow_share
    spreads = jax.random.uniform(gradual_random_key, (RANGE_BLOCKS, F, Q), minval=0.5, maxval=1.5)
    slow_rates = jnp.power(0.1, spreads / (2.0 * RANGE_BLOCKS))
    fast_rates = jax.random.uniform(quick_random_key, (RANGE_BLOCKS, F, Q), minval=0.02, maxval=0.1)
    spike_rows = jax.random.randint(spike_random_key, (3,), 0, RANGE_BLOCKS)
    spiking_active = jnp.any(jnp.arange(RANGE_BLOCKS)[:, None] == spike_rows[None, :], axis=1)[:, None, None]
    depths = jax.random.uniform(depth_random_key, (RANGE_BLOCKS, F, Q), minval=0.5, maxval=0.8)
    slow_rates = jnp.where(spiking_active, slow_rates * depths, slow_rates)
    return jnp.where(lasting, slow_rates, fast_rates).astype(jnp.float32)


def steps_of(stream_key, extent, cuts, low, largest):
    loudness, own = 1.0, jax.random.fold_in(stream_key, 6)
    for axis_at, shards_of in cuts:
        steps = jnp.exp(jax.random.uniform(jax.random.fold_in(own, axis_at), (shards_of,), jnp.float32, low / len(cuts), largest / len(cuts)))
        loudness = loudness * jnp.repeat(steps, extent[axis_at] // shards_of).reshape([-1 if axis == axis_at else 1 for axis in range(len(extent))])
    return loudness


def bell_draw(own_key, dims, scale, most, shards=(), kind=jnp.bfloat16):
    values = jax.random.normal(own_key, dims, jnp.float32) * scale
    if len(shards) > 0:
        values = steps_of(own_key, dims, shards, -0.22, 0.18) * values
    return jnp.clip(values, min=-most, max=most).astype(kind)


def setup_inputs(seed: int = 0) -> dict:
    splits = jax.random.split(jax.random.key(seed), 9)
    incident = bell_draw(splits[0], (2 * F, NR, NC), 1.0, 6.0, ((1, 32), (2, 16)), jnp.float32)
    inverse_diag = bell_draw(splits[1], (2 * F, NR, NC), 0.7, 4.0, ((1, 32), (2, 16)), jnp.float32)
    previous = bell_draw(splits[2], (2 * F, NR, NC), 0.5, 4.0, ((1, 32), (2, 16)), jnp.float32)
    heights = draw_heights(jax.random.fold_in(splits[8], 71), 0)
    neighbours = draw_neighbours(jax.random.fold_in(splits[8], 71), 0)
    counts = draw_counts(jax.random.fold_in(splits[8], 71), 0)
    transmit = draw_transmit(jax.random.fold_in(splits[8], 71), 0)
    angle_weights = bell_draw(splits[7], (F, 2, Q), 0.03, 0.15, (), jnp.float32)
    return dict(incident=incident, inverse_diag=inverse_diag, previous=previous, heights=heights, neighbours=neighbours, counts=counts, transmit=transmit, angle_weights=angle_weights)


green_scale = 0.25
phase_period = 64
highest_precision = lax.Precision.HIGHEST

def wave_tables(frequency, direction, row_ids, col_ids, block_heights):
    angle_ids = jnp.arange(Q, dtype=jnp.int32)
    range_step = direction * (1 + angle_ids // 8 + 2 * frequency)
    cross_step = angle_ids % 8 - 4 + frequency
    height_lift = 0.3 + 0.2 * frequency + 0.03 * angle_ids.astype(jnp.float32)
    phase_turns = (range_step[:, None, None] * row_ids[None, :, None] + cross_step[:, None, None] * col_ids[None, None, :]) % phase_period
    phase_angle = phase_turns.astype(jnp.float32) * (2.0 * math.pi / phase_period) + height_lift[:, None, None] * block_heights[None]
    return (jnp.cos(phase_angle), jnp.sin(phase_angle))

def decode_offsets(offset_codes):
    full_code = offset_codes + (offset_codes >= OFFSETS // 2).astype(jnp.int32)
    return (full_code // (2 * H + 1) - H, full_code % (2 * H + 1) - H)

def green_terms(distance, weight_live):
    pieces = []
    for frequency in range(F):
        wavenum = 0.5 * math.pi * (1.0 + 0.25 * frequency)
        magnitude = weight_live * green_scale / distance
        pieces.append(magnitude * jnp.cos(wavenum * distance))
        pieces.append(magnitude * jnp.sin(wavenum * distance))
    return jnp.stack(pieces)

def complex_apply(coupling, values):
    pieces = []
    for frequency in range(F):
        real_c = coupling[2 * frequency]
        imag_c = coupling[2 * frequency + 1]
        real_v = values[2 * frequency]
        imag_v = values[2 * frequency + 1]
        pieces.append(real_c * real_v - imag_c * imag_v)
        pieces.append(real_c * imag_v + imag_c * real_v)
    return jnp.stack(pieces)

def near_field(field, heights, neighbours, counts):
    width_pad = NC + 2 * H
    padded_field = jnp.pad(field, ((0, 0), (H, H), (H, H))).reshape(2 * F, -1)
    padded_heights = jnp.pad(heights, H).reshape(-1)
    anchor = ((jnp.arange(NR, dtype=jnp.int32)[:, None] + H) * width_pad + jnp.arange(NC, dtype=jnp.int32)[None, :] + H).astype(jnp.int32)

    def add_slot(running, slot_data):
        slot_codes, slot_index = slot_data
        shift_rows, shift_cols = decode_offsets(slot_codes)
        source_ids = (anchor + shift_rows * width_pad + shift_cols).astype(jnp.int32)
        other_heights = jnp.take(padded_heights, source_ids)
        distance = jnp.sqrt((shift_rows * shift_rows + shift_cols * shift_cols).astype(jnp.float32) + (other_heights - heights) ** 2)
        live_slot = (slot_index < counts).astype(jnp.float32)
        coupling = green_terms(distance, live_slot)
        gathered = jnp.take(padded_field, source_ids, axis=1)
        return (running + complex_apply(coupling, gathered), None)
    start_total = jnp.zeros((2 * F, NR, NC), jnp.float32)
    slot_indices = jnp.arange(LMAX, dtype=jnp.int32)
    total_field, _ = lax.scan(add_slot, start_total, (neighbours, slot_indices))
    return total_field

def reference(incident, inverse_diag, previous, heights, neighbours, counts, transmit, angle_weights):
    spread = 1.0 / math.sqrt(RD * NC)
    col_ids = jnp.arange(NC, dtype=jnp.int32)
    block_ids = jnp.arange(RANGE_BLOCKS, dtype=jnp.int32)

    def by_block(array):
        return jnp.moveaxis(array.reshape(array.shape[0], RANGE_BLOCKS, RD, NC), 1, 0)

    def unblock(array):
        return jnp.moveaxis(array, 0, 1).reshape(2 * F, NR, NC)
    height_blocks = heights.reshape(RANGE_BLOCKS, RD, NC)

    def weak_field(frequency, direction, row_ids, block_heights, carried):
        cos_wave, sin_wave = wave_tables(frequency, direction, row_ids, col_ids, block_heights)
        real_w = angle_weights[frequency, 0]
        imag_w = angle_weights[frequency, 1]
        real_s = carried[frequency, 0]
        imag_s = carried[frequency, 1]
        amp_real = real_w * real_s - imag_w * imag_s
        amp_imag = real_w * imag_s + imag_w * real_s
        field_real = spread * (jnp.einsum('a,arc->rc', amp_real, cos_wave, precision=highest_precision) - jnp.einsum('a,arc->rc', amp_imag, sin_wave, precision=highest_precision))
        field_imag = spread * (jnp.einsum('a,arc->rc', amp_real, sin_wave, precision=highest_precision) + jnp.einsum('a,arc->rc', amp_imag, cos_wave, precision=highest_precision))
        return (cos_wave, sin_wave, field_real, field_imag)

    def gather_back(cos_wave, sin_wave, flow_real, flow_imag):
        gain_real = jnp.einsum('arc,rc->a', cos_wave, flow_real, precision=highest_precision) + jnp.einsum('arc,rc->a', sin_wave, flow_imag, precision=highest_precision)
        gain_imag = jnp.einsum('arc,rc->a', cos_wave, flow_imag, precision=highest_precision) - jnp.einsum('arc,rc->a', sin_wave, flow_real, precision=highest_precision)
        return jnp.stack([gain_real, gain_imag])
    near_old = near_field(previous, heights, neighbours, counts)

    def forward_step(carried, block_data):
        block_id, fed_block, inverse_block, near_block, block_heights, decay = block_data
        row_ids = (block_id * RD + jnp.arange(RD, dtype=jnp.int32)).astype(jnp.int32)
        flows = []
        weak_parts = []
        renewed = []
        for frequency in range(F):
            cos_wave, sin_wave, field_real, field_imag = weak_field(frequency, 1, row_ids, block_heights, carried)
            rest_real = fed_block[2 * frequency] - near_block[2 * frequency] - field_real
            rest_imag = fed_block[2 * frequency + 1] - near_block[2 * frequency + 1] - field_imag
            inv_real = inverse_block[2 * frequency]
            inv_imag = inverse_block[2 * frequency + 1]
            flow_real = inv_real * rest_real - inv_imag * rest_imag
            flow_imag = inv_real * rest_imag + inv_imag * rest_real
            gained = gather_back(cos_wave, sin_wave, flow_real, flow_imag)
            renewed.append(decay[frequency] * (carried[frequency] + gained))
            flows += [flow_real, flow_imag]
            weak_parts += [field_real, field_imag]
        return (jnp.stack(renewed), (jnp.stack(flows), jnp.stack(weak_parts)))
    start_carry = jnp.zeros((F, 2, Q), jnp.float32)
    _, (forward_blocks, weak_blocks) = lax.scan(forward_step, start_carry, (block_ids, by_block(incident), by_block(inverse_diag), by_block(near_old), height_blocks, transmit))
    forward_currents = unblock(forward_blocks)
    near_new = near_field(forward_currents, heights, neighbours, counts)

    def backward_step(carried, block_data):
        block_id, fed_block, inverse_block, near_block, block_heights, decay, weak_block = block_data
        row_ids = (block_id * RD + jnp.arange(RD, dtype=jnp.int32)).astype(jnp.int32)
        flows = []
        renewed = []
        for frequency in range(F):
            inv_real = inverse_block[2 * frequency]
            inv_imag = inverse_block[2 * frequency + 1]
            rest_real = fed_block[2 * frequency] - near_block[2 * frequency] - weak_block[2 * frequency]
            rest_imag = fed_block[2 * frequency + 1] - near_block[2 * frequency + 1] - weak_block[2 * frequency + 1]
            driven_real = inv_real * rest_real - inv_imag * rest_imag
            driven_imag = inv_real * rest_imag + inv_imag * rest_real
            cos_wave, sin_wave, field_real, field_imag = weak_field(frequency, -1, row_ids, block_heights, carried)
            flow_real = driven_real - (inv_real * field_real - inv_imag * field_imag)
            flow_imag = driven_imag - (inv_real * field_imag + inv_imag * field_real)
            gained = gather_back(cos_wave, sin_wave, flow_real, flow_imag)
            renewed.append(decay[frequency] * (carried[frequency] + gained))
            flows += [flow_real, flow_imag]
        return (jnp.stack(renewed), jnp.stack(flows))
    _, backward_blocks = lax.scan(backward_step, start_carry, (block_ids, by_block(incident), by_block(inverse_diag), by_block(near_new), height_blocks, transmit, weak_blocks), reverse=True)
    currents = unblock(backward_blocks)
    return (forward_currents, currents)
```

```python
import functools
import math

import jax
import jax.numpy as jnp
import numpy as np
from jax import lax
from jax.experimental import pallas as pl
from jax.experimental.pallas import tpu as pltpu
from jax.sharding import PartitionSpec as P

F = 2
Q = 64
H = 3
LMAX = 24
RD = 16
XD = 128
SIDE = 2 * H + 1
MESH = pl.DeviceIdType.MESH
f32 = jnp.float32
bf16 = jnp.bfloat16
i32 = jnp.int32


def phase_tables():
    turn = 2.0 * math.pi / 64
    power = np.arange(16) - 7
    cols = np.arange(XD)
    ang = turn * ((power[:, None] * cols[None, :]) % 64)
    v_rows = np.stack([np.cos(ang), np.sin(ang)]).astype(np.float32)
    u_rows = np.zeros((4, RD, 2, 16, XD), np.float32)
    cell = np.zeros((4, 12, RD, XD), np.float32)
    for dm in range(4):
        rows = 16 * dm + np.arange(RD)
        ang = turn * ((power[None, :] * rows[:, None]) % 64)
        u_rows[dm, :, 0] = np.cos(ang)[:, :, None]
        u_rows[dm, :, 1] = np.sin(ang)[:, :, None]
        for way, sign in enumerate((1, -1)):
            for f in range(F):
                ang = turn * ((sign * (1 + 2 * f) * rows[:, None] + (f - 4) * cols[None, :]) % 64)
                cell[dm, way * 4 + f * 2] = np.cos(ang)
                cell[dm, way * 4 + f * 2 + 1] = np.sin(ang)
        ang = turn * ((rows[:, None] + 0 * cols[None, :]) % 64)
        cell[dm, 8], cell[dm, 9] = np.cos(ang), np.sin(ang)
        ang = turn * ((0 * rows[:, None] + cols[None, :]) % 64)
        cell[dm, 10], cell[dm, 11] = np.cos(ang), np.sin(ang)
    return v_rows, u_rows, cell


def sincos_small(t):
    q = t * t
    s = t * (1.0 + q * (-1.0 / 6 + q * (1.0 / 120 + q * (-1.0 / 5040 + q * (1.0 / 362880)))))
    c = 1.0 + q * (-0.5 + q * (1.0 / 24 + q * (-1.0 / 720 + q * (1.0 / 40320))))
    return s, c


def sincos(t):
    q = t * t
    s = t * (
        1.0
        + q
        * (
            -1.0 / 6
            + q * (1.0 / 120 + q * (-1.0 / 5040 + q * (1.0 / 362880 + q * (-1.0 / 39916800))))
        )
    )
    c = 1.0 + q * (
        -0.5
        + q
        * (
            1.0 / 24
            + q
            * (-1.0 / 720 + q * (1.0 / 40320 + q * (-1.0 / 3628800 + q * (1.0 / 479001600))))
        )
    )
    return s, c


def squared(c, s):
    return c * c - s * s, 2.0 * (c * s)


def lanes_of(shape):
    return lax.broadcasted_iota(i32, shape, 1)


def rows_of(shape):
    return lax.broadcasted_iota(i32, shape, 0)


def pick(value, index):
    return jnp.take_along_axis(value, index, axis=1, mode="promise_in_bounds")


def split(value):
    high = value.astype(bf16)
    return high, (value - high.astype(f32)).astype(bf16)


def contract(left, right):
    return lax.dot_general(left, right, (((1,), (1,)), ((), ())), preferred_element_type=f32)


def contract3(left_high, left_low, right_high, right_low):
    return (
        contract(left_high, right_high)
        + contract(left_high, right_low)
        + contract(left_low, right_high)
    )


def regroup(value):
    shape = (8, 128)
    part = (rows_of(shape) - lanes_of(shape) // 16) & 7
    out = jnp.zeros(shape, f32)
    for s in range(8):
        moved = value
        if s:
            moved = pltpu.roll(pltpu.roll(value, 128 - 16 * s, 1), s, 0)
        out = jnp.where(part == s, moved, out)
    return out


def kernel(
    nd, nx,
    inc, zin, prev, hts, nbr, cnt, trn, aw, v_rows, u_hbm, cell_hbm,
    out_f, out_c,
    u_rows, cell, cbuf, edge_l, edge_r, pk_l, pk_r,
    cbuf2, edge_l2, edge_r2, pk_l2, pk_r2,
    shifted, table, tab_u_h, tab_u_l, tab_a_h, tab_a_l, tab_v, tab_f_h, tab_f_l,
    srcp, loaded, driven, weakf, w_lane, w_sub, row_buf,
    gx, gmsg, gr, fx, fx2, fmsg, fmsg2, fr, mats, state,
    base, vu,
    csem, hs_sem, hr_sem, hs2_sem, hr2_sem,
    gxs, gxr, grs, grr, fxs, fxr, fxs2, fxr2, frs, frr,
):
    d = lax.axis_index("rng")
    x = lax.axis_index("xr")
    dm = lax.rem(d, 4)
    spread = 1.0 / math.sqrt(RD * XD * nx)
    up, down = lax.rem(d + nd - 1, nd), lax.rem(d + 1, nd)
    left, right = lax.rem(x + nx - 1, nx), lax.rem(x + 1, nx)

    cu = pltpu.make_async_copy(u_hbm.at[dm], u_rows, csem.at[0])
    cc = pltpu.make_async_copy(cell_hbm.at[dm], cell, csem.at[1])
    cu.start()
    cc.start()

    barrier = pltpu.get_barrier_semaphore()

    def greet_rng(off, carry):
        pl.semaphore_signal(barrier, inc=1, device_id=(lax.rem(d + off, nd), x), device_id_type=MESH)
        return carry

    def greet_xr(off, carry):
        pl.semaphore_signal(barrier, inc=1, device_id=(d, lax.rem(x + off, nx)), device_id_type=MESH)
        return carry

    lax.fori_loop(1, nd, greet_rng, 0)
    lax.fori_loop(1, nx, greet_xr, 0)
    for dd in (up, down):
        for xx in (left, right):
            pl.semaphore_signal(barrier, inc=1, device_id=(dd, xx), device_id_type=MESH)

    wide = (RD, XD)
    lane16 = lanes_of(wide)
    small = (8, 128)
    lane8 = lanes_of(small)
    sub8 = rows_of(small)

    def pack_edges(parts, to_left, to_right):
        a = jnp.zeros(wide, f32)
        b = jnp.zeros(wide, f32)
        for c, part in enumerate(parts):
            here = lane16 // 8 == c
            a = jnp.where(here, part if c == 0 else pltpu.roll(part, 8 * c, 1), a)
            b = jnp.where(here, pltpu.roll(part, 8 * c + 3, 1), b)
        to_left[...] = a
        to_right[...] = b

    for c in range(4):
        cbuf[c, 8:24, :] = prev[c]
    cbuf[4, 8:24, :] = hts[...]
    pack_edges([prev[0], prev[1], prev[2], prev[3], hts[...]], pk_l, pk_r)
    zero8 = jnp.zeros(small, f32)
    for slot in (0, nd + 1):
        gr[slot] = zero8
        fr[slot] = zero8

    pl.semaphore_wait(barrier, nd - 1 + nx - 1 + 4)

    def halo(buf, e_l, e_r, p_l, p_r, send, recv):
        plan = [
            (buf.at[:, 8:16, :], buf.at[:, 24:32, :], (up, x)),
            (buf.at[:, 16:24, :], buf.at[:, 0:8, :], (down, x)),
            (p_l, e_r.at[8:24, :], (d, left)),
            (p_r, e_l.at[8:24, :], (d, right)),
            (p_l.at[0:8, :], e_r.at[24:32, :], (up, left)),
            (p_l.at[8:16, :], e_r.at[0:8, :], (down, left)),
            (p_r.at[0:8, :], e_l.at[24:32, :], (up, right)),
            (p_r.at[8:16, :], e_l.at[0:8, :], (down, right)),
        ]
        return [
            pltpu.make_async_remote_copy(
                src_ref=src, dst_ref=dst, send_sem=send.at[n], recv_sem=recv.at[n],
                device_id=dev, device_id_type=MESH,
            )
            for n, (src, dst, dev) in enumerate(plan)
        ]

    halo1 = halo(cbuf, edge_l, edge_r, pk_l, pk_r, hs_sem, hr_sem)
    for copy in halo1:
        copy.start()

    cu.wait()
    power16 = (rows_of(wide) - 7).astype(f32) * 0.03

    def fill(r, carry):
        at = pl.ds(pl.multiple_of(r * XD, XD), XD)
        hrow = jnp.broadcast_to(hts[pl.ds(r, 1), :], wide)
        hs, hc = sincos_small(power16 * hrow)
        vc0, vs0 = v_rows[0], v_rows[1]
        vc = hc * vc0 - hs * vs0
        vs = hc * vs0 + hs * vc0
        tab_v[0, :, at] = vc[:8]
        tab_v[1, :, at] = vs[:8]
        c8, s8 = squared(*squared(*squared(hc, hs)))
        pc, ps = u_rows[r, 0], u_rows[r, 1]
        cc_, ss_, cs_, sc_ = c8 * pc, s8 * ps, c8 * ps, s8 * pc
        for n, value in enumerate((cc_ - ss_, sc_ + cs_, cc_ + ss_, sc_ - cs_)):
            high, low = split(value)
            tab_u_h[16 * n : 16 * n + 16, at] = high
            tab_u_l[16 * n : 16 * n + 16, at] = low
        for f in range(F):
            zr = jnp.broadcast_to(zin[2 * f, pl.ds(r, 1), :], wide)
            zi = jnp.broadcast_to(zin[2 * f + 1, pl.ds(r, 1), :], wide)
            for n, value in enumerate((zr * vc - zi * vs, zr * vs + zi * vc)):
                high, low = split(value)
                k = 2 * f + n
                tab_a_h[16 * k : 16 * k + 16, at] = high
                tab_a_l[16 * k : 16 * k + 16, at] = low
        return carry

    lax.fori_loop(0, RD, fill, 0)

    y = contract3(tab_u_h[...], tab_u_l[...], tab_a_h[...], tab_a_l[...])
    yc = jnp.concatenate([y[0:16], y[32:48]], axis=1)
    ys = jnp.concatenate([y[16:32], y[48:64]], axis=1)
    gx[x] = yc + jnp.where((lane16 // 16) % 2 == 0, -pltpu.roll(ys, 112, 1), pltpu.roll(ys, 16, 1))

    def spread_xr(buf, send, recv):
        def step(off, carry):
            pltpu.make_async_remote_copy(
                src_ref=buf.at[x], dst_ref=buf.at[x], send_sem=send, recv_sem=recv,
                device_id=(d, lax.rem(x + off, nx)), device_id_type=MESH,
            ).start()
            return carry

        lax.fori_loop(1, nx, step, 0)

    def await_bytes(view, sem):
        pltpu.make_async_copy(view, view, sem).wait()

    def total_xr(buf):
        total = buf[0]
        for k in range(1, nx):
            total = total + buf[k]
        return total

    spread_xr(gx, gxs, gxr)

    row_buf[...] = zero8
    for f in range(F):
        for c in range(2):
            row_buf[2 * f + c : 2 * f + c + 1, 0:Q] = aw[f, c : c + 1, :]
    row_buf[4:6, 0:Q] = trn[0]
    li, lj = lane8 // 16, lane8 % 16
    lane_rows = jnp.where(lj < 8, pick(row_buf[...], (li * 8 + lj) & 127), 0.0)
    for k in range(4):
        row = jnp.broadcast_to(lane_rows[k : k + 1, :], small) * spread
        w_lane[k] = row
        for i in range(8):
            w_sub[k, i] = pick(row, sub8 + 16 * i)

    cc.wait()
    hh = hts[...]
    hs, hc = sincos_small(0.03 * hh)
    c8, s8 = squared(*squared(*squared(hc, hs)))
    vu[0] = hc * cell[10] - hs * cell[11]
    vu[1] = hc * cell[11] + hs * cell[10]
    vu[2] = c8 * cell[8] - s8 * cell[9]
    vu[3] = s8 * cell[8] + c8 * cell[9]
    vu[4] = c8 * cell[8] + s8 * cell[9]
    vu[5] = s8 * cell[8] - c8 * cell[9]
    for f in range(F):
        s, c = sincos((0.3 + 0.2 * f) * hh)
        for way in range(2):
            k = way * 4 + f * 2
            base[k] = c * cell[k] - s * cell[k + 1]
            base[k + 1] = s * cell[k] + c * cell[k + 1]

    def note(l, words):
        word0, word1 = words
        code = nbr[l]
        m = jnp.where(code >= 24, code + 1, code)
        low = m < 28
        bit = jnp.where(l < cnt[...], jnp.left_shift(1, jnp.where(low, m, m - 28)), 0)
        return word0 | jnp.where(low, bit, 0), word1 | jnp.where(low, 0, bit)

    zero_word = jnp.zeros(wide, i32)
    words = lax.fori_loop(0, LMAX, note, (zero_word, zero_word))

    tall = (32, XD)
    lane32 = lanes_of(tall)
    row32 = rows_of(tall) + (d * RD - 8)
    inside = (row32 >= 0) & (row32 < nd * RD)

    def shift_all(buf, e_l, e_r, count):
        el = jnp.where(inside & (lane32 < 128 * x), e_l[...], 0.0)
        er = jnp.where(inside & (lane32 < 128 * (nx - 1 - x)), e_r[...], 0.0)
        for c in range(count):
            mid = jnp.where(inside, buf[c], 0.0)
            shifted[H, c] = mid
            for k in range(1, H + 1):
                shifted[H + k, c] = jnp.where(
                    lane32 >= 128 - k,
                    pltpu.roll(er, (128 - k - 8 * c) % 128, 1),
                    pltpu.roll(mid, 128 - k, 1),
                )
                shifted[H - k, c] = jnp.where(
                    lane32 < k,
                    pltpu.roll(el, (k - 3 - 8 * c) % 128, 1),
                    pltpu.roll(mid, k, 1),
                )

    def window(dyi, c, dx):
        return shifted[dyi, c, 8 + dx : 24 + dx, :]

    def applied(total, g, dyi, dx):
        out = []
        for f in range(F):
            gr_, gi_ = g[2 * f], g[2 * f + 1]
            ur, ui = window(dyi, 2 * f, dx), window(dyi, 2 * f + 1, dx)
            out.append(total[2 * f] + (gr_ * ur - gi_ * ui))
            out.append(total[2 * f + 1] + (gr_ * ui + gi_ * ur))
        return tuple(out)

    for copy in halo1:
        copy.wait_recv()
    shift_all(cbuf, edge_l, edge_r, 5)

    def couple(dyi, total):
        dy = dyi - H
        for dxi in range(SIDE):
            dx = dxi - H
            square = jnp.maximum(dx * dx + dy * dy, 1).astype(f32)
            rise = window(dyi, 4, dx) - hh
            dist2 = square + rise * rise
            inv = lax.rsqrt(dist2)
            inv = inv * (1.5 - 0.5 * dist2 * (inv * inv))
            bits = words[dxi // 4] >> (7 * (dxi % 4) + dyi)
            mag = jnp.where((bits & 1) == 1, 0.25 * inv, 0.0)
            s1, c1 = sincos((math.pi / 8) * (dist2 * inv) - 0.5 * math.pi)
            s1, c1 = c1, -s1
            c4, s4 = squared(*squared(c1, s1))
            g = (
                mag * c4,
                mag * s4,
                mag * (c4 * c1 - s4 * s1),
                mag * (s4 * c1 + c4 * s1),
            )
            for c in range(4):
                table[dyi, dxi, c] = g[c]
            total = applied(total, g, dyi, dx)
        return total

    def recouple(dyi, total):
        for dxi in range(SIDE):
            g = [table[dyi, dxi, c] for c in range(4)]
            total = applied(total, g, dyi, dxi - H)
        return total

    nothing = (jnp.zeros(wide, f32),) * 4
    near_old = lax.fori_loop(0, SIDE, couple, nothing)

    def times_z(f, real, imag):
        zr, zi = zin[2 * f], zin[2 * f + 1]
        return zr * real - zi * imag, zr * imag + zi * real

    def project(way, field, buf, send, recv):
        for f in range(F):
            k = way * 4 + f * 2
            br, bi = base[k], base[k + 1]
            sr, si = field[2 * f], field[2 * f + 1]
            srcp[2 * f] = br * sr + bi * si
            srcp[2 * f + 1] = br * si - bi * sr

        def lay(r, carry):
            at = pl.ds(pl.multiple_of(r * XD, XD), XD)
            vc, vs = tab_v[0, :, at], tab_v[1, :, at]
            for f in range(F):
                sr = jnp.broadcast_to(srcp[2 * f, pl.ds(r, 1), :], small)
                si = jnp.broadcast_to(srcp[2 * f + 1, pl.ds(r, 1), :], small)
                both = jnp.concatenate([sr * vc - si * vs, sr * vs + si * vc], axis=0)
                high, low = split(both)
                tab_f_h[16 * f : 16 * f + 16, at] = high
                tab_f_l[16 * f : 16 * f + 16, at] = low
            return carry

        lax.fori_loop(0, RD, lay, 0)
        rows = slice(32 * way, 32 * way + 32)
        y = contract3(tab_u_h[rows, :], tab_u_l[rows, :], tab_f_h[...], tab_f_l[...])
        pad = jnp.zeros((8, 96), f32)
        yc = jnp.concatenate([y[0:8], pad], axis=1)
        ys = jnp.concatenate([y[16:24], pad], axis=1)
        buf[x] = yc + jnp.where((lane8 // 8) % 2 == 0, -pltpu.roll(ys, 120, 1), pltpu.roll(ys, 8, 1))
        spread_xr(buf, send, recv)

    for f in range(F):
        sr, si = times_z(f, inc[2 * f] - near_old[2 * f], inc[2 * f + 1] - near_old[2 * f + 1])
        loaded[2 * f] = sr
        loaded[2 * f + 1] = si
    project(0, loaded, fx, fxs, fxr)

    await_bytes(gx.at[pl.ds(0, nx - 1)], gxr)
    g_sum = total_xr(gx)
    h0, h1 = regroup(g_sum[:8]), regroup(g_sum[8:])
    gmsg[0] = jnp.where(sub8 < 4, h0, pltpu.roll(h1, 4, 0))
    gmsg[1] = jnp.where(sub8 < 4, pltpu.roll(h0, 4, 0), h1)

    def send_g(off, carry):
        pltpu.make_async_remote_copy(
            src_ref=gmsg.at[(d + off) // nd], dst_ref=gr.at[d + 1],
            send_sem=grs, recv_sem=grr.at[d],
            device_id=(lax.rem(d + off, nd), x), device_id_type=MESH,
        ).start()
        return carry

    lax.fori_loop(1, nd, send_g, 0)

    def send_feed(buf, recv, msg, first, last):
        await_bytes(buf.at[pl.ds(0, nx - 1)], recv)
        total = total_xr(buf)
        out = lane_rows
        for k in range(4):
            spreadout = pick(total, (8 * k + 7 - lj) & 127)
            spreadout = jnp.where((sub8 == 7 - li) & (lj < 8), spreadout, 0.0)
            row = jnp.sum(spreadout, axis=0, keepdims=True)
            out = jnp.where(sub8 == k, jnp.broadcast_to(row, small), out)
        msg[...] = out

        def step(to, carry):
            pltpu.make_async_remote_copy(
                src_ref=msg, dst_ref=fr.at[d + 1], send_sem=frs, recv_sem=frr.at[d],
                device_id=(to, x), device_id_type=MESH,
            ).start()
            return carry

        lax.fori_loop(first, last, step, 0)

    def await_slots(buf, sem, first, last):
        def step(k, carry):
            await_bytes(buf.at[k + 1], sem.at[k])
            return carry

        lax.fori_loop(first, last, step, 0)

    def build(slot, first):
        if first:
            start = (7 - li) * 16 + sub8 - lj + 7
        else:
            start = (li + 7) * 16 + lj - sub8 + 7
        for f in range(F):
            half = [
                [jnp.broadcast_to(gr[slot, r : r + 1, :], small) for r in (2 * f + c, 4 + 2 * f + c)]
                for c in range(2)
            ]
            for i in range(8):
                src = start + 16 * i if first else start - 16 * i
                index = src & 127
                near = src < 128
                mr = jnp.where(near, pick(half[0][0], index), pick(half[0][1], index))
                mi = jnp.where(near, pick(half[1][0], index), pick(half[1][1], index))
                own = lane8 == sub8 + 16 * i
                if first:
                    wr, wi = w_sub[2 * f, i], w_sub[2 * f + 1, i]
                else:
                    wr, wi = w_lane[2 * f], w_lane[2 * f + 1]
                    own = own | (lane8 == sub8 + (16 * i + 8))
                mats[slot, f, 0, i] = jnp.where(own, 1.0, 0.0) - (mr * wr - mi * wi)
                mats[slot, f, 1, i] = -(mr * wi + mi * wr)

    def slots_of(way, t):
        if way == 0:
            at = 2 * t - lax.rem(d, 2)
            return at + 1, at + 2
        at = 2 * t - lax.rem(nd - 1 - d, 2)
        return nd - at, nd - at - 1

    def pairs_of(way):
        return (d + 1) // 2 if way == 0 else (nd - d) // 2

    def build_all(way):
        if way == 0:
            await_slots(gr, grr, 0, d)
        else:
            await_slots(gr, grr, d + 1, nd)

        def step(t, carry):
            one, two = slots_of(way, t)
            build(one, True)
            build(two, False)
            return carry

        lax.fori_loop(0, pairs_of(way), step, 0)

    def sweep(way):
        if way == 0:
            await_slots(fr, frr, 0, d)
        else:
            await_slots(fr, frr, d + 1, nd)
        for f in range(F):
            for c in range(2):
                for i in range(8):
                    state[f, c, i] = zero8

        def row(slot, k):
            return jnp.broadcast_to(fr[slot, k : k + 1, :], small)

        def step(t, carry):
            one, two = slots_of(way, t)
            for f in range(F):
                ar = ai = zero8
                for i in range(8):
                    mr, mi = mats[one, f, 0, i], mats[one, f, 1, i]
                    sr, si = state[f, 0, i], state[f, 1, i]
                    ar = ar + (mr * sr - mi * si)
                    ai = ai + (mr * si + mi * sr)
                share = row(one, 4 + f)
                yr = share * (jnp.sum(ar, axis=0, keepdims=True) + row(one, 2 * f))
                yi = share * (jnp.sum(ai, axis=0, keepdims=True) + row(one, 2 * f + 1))
                yr = yr + pltpu.roll(row(two, 2 * f), 8, 1)
                yi = yi + pltpu.roll(row(two, 2 * f + 1), 8, 1)
                share = row(two, 4 + f)
                for i in range(8):
                    mr, mi = mats[two, f, 0, i], mats[two, f, 1, i]
                    own = pick(share, sub8 + 16 * i)
                    vr = jnp.sum(mr * yr - mi * yi, axis=1, keepdims=True)
                    vi = jnp.sum(mr * yi + mi * yr, axis=1, keepdims=True)
                    state[f, 0, i] = own * vr
                    state[f, 1, i] = own * vi
            return carry

        lax.fori_loop(0, pairs_of(way), step, 0)

    def radiate(way):
        for f in range(F):
            for i in range(8):
                wr, wi = w_sub[2 * f, i], w_sub[2 * f + 1, i]
                sr, si = state[f, 0, i], state[f, 1, i]
                state[f, 0, i] = wr * sr - wi * si
                state[f, 1, i] = wr * si + wi * sr
        vr, vi = vu[0], vu[1]
        ur, ui = vu[2 + 2 * way], vu[3 + 2 * way]

        def step(n, total):
            i = 7 - n
            out = []
            for f in range(F):
                tr, ti = total[2 * f], total[2 * f + 1]

                def coef(c, j):
                    return jnp.broadcast_to(state[f, c, i, j : j + 1, :], wide)

                ar, ai = coef(0, 7), coef(1, 7)
                for j in range(6, -1, -1):
                    ar, ai = ar * vr - ai * vi + coef(0, j), ar * vi + ai * vr + coef(1, j)
                out += [tr * ur - ti * ui + ar, tr * ui + ti * ur + ai]
            return tuple(out)

        total = lax.fori_loop(0, 8, step, nothing)
        out = []
        for f in range(F):
            k = way * 4 + f * 2
            br, bi = base[k], base[k + 1]
            tr, ti = total[2 * f], total[2 * f + 1]
            out += [br * tr - bi * ti, br * ti + bi * tr]
        return out

    send_feed(fx, fxr, fmsg, d + 1, nd)
    build_all(0)
    sweep(0)
    weak = radiate(0)
    flow = []
    for f in range(F):
        ar, ai = times_z(f, weak[2 * f], weak[2 * f + 1])
        flow += [loaded[2 * f] - ar, loaded[2 * f + 1] - ai]
    for c in range(4):
        out_f[c] = flow[c]
        cbuf2[c, 8:24, :] = flow[c]
        weakf[c] = weak[c]
    pack_edges(flow, pk_l2, pk_r2)
    halo2 = halo(cbuf2, edge_l2, edge_r2, pk_l2, pk_r2, hs2_sem, hr2_sem)
    for copy in halo2:
        copy.start()

    build_all(1)
    for copy in halo2:
        copy.wait_recv()
    shift_all(cbuf2, edge_l2, edge_r2, 4)
    near_new = lax.fori_loop(0, SIDE, recouple, nothing)
    for f in range(F):
        dr, di = times_z(
            f,
            inc[2 * f] - near_new[2 * f] - weakf[2 * f],
            inc[2 * f + 1] - near_new[2 * f + 1] - weakf[2 * f + 1],
        )
        driven[2 * f] = dr
        driven[2 * f + 1] = di
    project(1, driven, fx2, fxs2, fxr2)
    send_feed(fx2, fxr2, fmsg2, 0, d)
    sweep(1)
    weak = radiate(1)
    for f in range(F):
        ar, ai = times_z(f, weak[2 * f], weak[2 * f + 1])
        out_c[2 * f] = driven[2 * f] - ar
        out_c[2 * f + 1] = driven[2 * f + 1] - ai

    for copy in halo1 + halo2:
        copy.wait_send()
    await_bytes(gx.at[pl.ds(0, nx - 1)], gxs)
    await_bytes(fx.at[pl.ds(0, nx - 1)], fxs)
    await_bytes(fx2.at[pl.ds(0, nx - 1)], fxs2)
    await_bytes(gr.at[pl.ds(0, nd - 1)], grs)
    await_bytes(fr.at[pl.ds(0, nd - 1)], frs)


def solution(mesh):
    nd, nx = mesh.shape["rng"], mesh.shape["xr"]
    v_rows, u_rows, cell = phase_tables()

    def per_device(incident, inverse_diag, previous, heights, neighbours, counts, transmit, angle_weights):
        vmem = pl.BlockSpec(memory_space=pltpu.VMEM)
        anywhere = pl.BlockSpec(memory_space=pl.ANY)
        points = RD * XD
        block = jax.ShapeDtypeStruct((2 * F, RD, XD), f32)
        V = pltpu.VMEM
        dma = pltpu.SemaphoreType.DMA
        scratch = [
            V((RD, 2, 16, XD), f32), V((12, RD, XD), f32),
            V((5, 32, XD), f32), V((32, XD), f32), V((32, XD), f32), V((RD, XD), f32), V((RD, XD), f32),
            V((4, 32, XD), f32), V((32, XD), f32), V((32, XD), f32), V((RD, XD), f32), V((RD, XD), f32),
            V((SIDE, 5, 32, XD), f32), V((SIDE, SIDE, 4, RD, XD), f32),
            V((64, points), bf16), V((64, points), bf16), V((64, points), bf16), V((64, points), bf16),
            V((2, 8, points), f32), V((32, points), bf16), V((32, points), bf16),
            V((4, RD, XD), f32), V((4, RD, XD), f32), V((4, RD, XD), f32), V((4, RD, XD), f32),
            V((4, 8, 128), f32), V((4, 8, 8, 128), f32), V((8, 128), f32),
            V((nx, 16, 128), f32), V((2, 8, 128), f32), V((nd + 2, 8, 128), f32),
            V((nx, 8, 128), f32), V((nx, 8, 128), f32), V((8, 128), f32), V((8, 128), f32),
            V((nd + 2, 8, 128), f32), V((nd + 2, F, 2, 8, 8, 128), f32), V((F, 2, 8, 8, 128), f32),
            V((8, RD, XD), f32), V((6, RD, XD), f32),
            dma((2,)), dma((8,)), dma((8,)), dma((8,)), dma((8,)),
            dma, dma, dma, dma((nd,)), dma, dma, dma, dma, dma, dma((nd,)),
        ]
        return pl.pallas_call(
            functools.partial(kernel, nd, nx),
            out_shape=(block, block),
            in_specs=[vmem] * 9 + [anywhere] * 2,
            out_specs=(vmem, vmem),
            scratch_shapes=scratch,
            compiler_params=pltpu.CompilerParams(
                collective_id=0, has_side_effects=True, vmem_limit_bytes=40 << 20
            ),
        )(
            incident, inverse_diag, previous, heights, neighbours, counts, transmit, angle_weights,
            jnp.asarray(v_rows), jnp.asarray(u_rows), jnp.asarray(cell),
        )

    placed = (
        P(None, "rng", "xr"),
        P(None, "rng", "xr"),
        P(None, "rng", "xr"),
        P("rng", "xr"),
        P(None, "rng", "xr"),
        P("rng", "xr"),
        P("rng", None, None),
        P(),
    )
    return jax.shard_map(
        per_device,
        mesh=mesh,
        in_specs=placed,
        out_specs=(P(None, "rng", "xr"), P(None, "rng", "xr")),
        check_vma=False,
    )
```

```python
import functools
import math

import jax
import jax.numpy as jnp
import numpy as np
from jax import lax
from jax.experimental import pallas as pl
from jax.experimental.pallas import tpu as pltpu
from jax.sharding import PartitionSpec as P

F = 2
Q = 64
H = 3
LMAX = 24
RD = 16
XD = 128
SIDE = 2 * H + 1
MESH = pl.DeviceIdType.MESH
f32 = jnp.float32
bf16 = jnp.bfloat16
i32 = jnp.int32


def phase_tables():
    turn = 2.0 * math.pi / 64
    power = np.arange(16) - 7
    cols = np.arange(XD)
    ang = turn * ((power[:, None] * cols[None, :]) % 64)
    v_rows = np.stack([np.cos(ang), np.sin(ang)]).astype(np.float32)
    u_rows = np.zeros((4, RD, 2, 16, XD), np.float32)
    cell = np.zeros((4, 12, RD, XD), np.float32)
    for dm in range(4):
        rows = 16 * dm + np.arange(RD)
        ang = turn * ((power[None, :] * rows[:, None]) % 64)
        u_rows[dm, :, 0] = np.cos(ang)[:, :, None]
        u_rows[dm, :, 1] = np.sin(ang)[:, :, None]
        for way, sign in enumerate((1, -1)):
            for f in range(F):
                ang = turn * ((sign * (1 + 2 * f) * rows[:, None] + (f - 4) * cols[None, :]) % 64)
                cell[dm, way * 4 + f * 2] = np.cos(ang)
                cell[dm, way * 4 + f * 2 + 1] = np.sin(ang)
        ang = turn * ((rows[:, None] + 0 * cols[None, :]) % 64)
        cell[dm, 8], cell[dm, 9] = np.cos(ang), np.sin(ang)
        ang = turn * ((0 * rows[:, None] + cols[None, :]) % 64)
        cell[dm, 10], cell[dm, 11] = np.cos(ang), np.sin(ang)
    return v_rows, u_rows, cell


def sincos_small(t):
    q = t * t
    s = t * (1.0 + q * (-1.0 / 6 + q * (1.0 / 120 + q * (-1.0 / 5040 + q * (1.0 / 362880)))))
    c = 1.0 + q * (-0.5 + q * (1.0 / 24 + q * (-1.0 / 720 + q * (1.0 / 40320))))
    return s, c


def sincos(t):
    q = t * t
    s = t * (
        1.0
        + q
        * (
            -1.0 / 6
            + q * (1.0 / 120 + q * (-1.0 / 5040 + q * (1.0 / 362880 + q * (-1.0 / 39916800))))
        )
    )
    c = 1.0 + q * (
        -0.5
        + q
        * (
            1.0 / 24
            + q
            * (-1.0 / 720 + q * (1.0 / 40320 + q * (-1.0 / 3628800 + q * (1.0 / 479001600))))
        )
    )
    return s, c


def squared(c, s):
    return c * c - s * s, 2.0 * (c * s)


def lanes_of(shape):
    return lax.broadcasted_iota(i32, shape, 1)


def rows_of(shape):
    return lax.broadcasted_iota(i32, shape, 0)


def pick(value, index):
    return jnp.take_along_axis(value, index, axis=1, mode="promise_in_bounds")


def split(value):
    high = value.astype(bf16)
    return high, (value - high.astype(f32)).astype(bf16)


def contract(left, right):
    return lax.dot_general(left, right, (((1,), (1,)), ((), ())), preferred_element_type=f32)


def contract3(left_high, left_low, right_high, right_low):
    return (
        contract(left_high, right_high)
        + contract(left_high, right_low)
        + contract(left_low, right_high)
    )


def regroup(value):
    shape = (8, 128)
    part = (rows_of(shape) - lanes_of(shape) // 16) & 7
    out = jnp.zeros(shape, f32)
    for s in range(8):
        moved = value
        if s:
            moved = pltpu.roll(pltpu.roll(value, 128 - 16 * s, 1), s, 0)
        out = jnp.where(part == s, moved, out)
    return out


def kernel(
    nd, nx,
    inc_hbm, zin_hbm, prev_hbm, hts_hbm, nbr_hbm, cnt_hbm, trn_hbm, aw_hbm, v_hbm, u_hbm, cell_hbm,
    out_f, out_c,
    inc, zin, prev, hts, nbr, cnt, trn, aw, v_rows, u_rows, cell, cbuf, edge_l, edge_r, pk_l, pk_r,
    cbuf2, edge_l2, edge_r2, pk_l2, pk_r2,
    shifted, table, tab_u_h, tab_u_l, tab_a_h, tab_a_l, tab_v, tab_f_h, tab_f_l,
    srcp, loaded, driven, weakf, w_lane, w_sub, row_buf, share_msg, tr,
    gx, gmsg, gr, fx, fx2, fmsg, fmsg2, fr, mats, state,
    base, vu,
    csem, hs_sem, hr_sem, hs2_sem, hr2_sem,
    gxs, gxr, grs, grr, fxs, fxr, fxs2, fxr2, frs, frr, trs, trr,
):
    d = lax.axis_index("rng")
    x = lax.axis_index("xr")
    dm = lax.rem(d, 4)
    spread = 1.0 / math.sqrt(RD * XD * nx)
    up, down = lax.rem(d + nd - 1, nd), lax.rem(d + 1, nd)
    left, right = lax.rem(x + nx - 1, nx), lax.rem(x + 1, nx)

    def turned(value, by, size):
        moved = value + by
        return jnp.where(moved >= size, moved - size, moved)

    nc = min(4, nd)
    nr = nd // nc
    far = lambda n, size: min(n, size - n)
    others = sorted(
        ((a, b) for a in range(nr) for b in range(nc) if a or b),
        key=lambda p: -far(p[0], nr) - far(p[1], nc),
    )
    d_row, d_col = d // nc, lax.rem(d, nc)
    blocks = [turned(d_row, a, nr) * nc + turned(d_col, b, nc) for a, b in others]
    owners = [turned(x, n, nx) for n in sorted(range(1, nx), key=lambda n: -far(n, nx))]

    barrier = pltpu.get_barrier_semaphore()
    peers = [(to, x) for to in blocks] + [(d, to) for to in owners]
    peers += [(dd, xx) for dd in (up, down) for xx in (left, right)]
    for peer in peers:
        pl.semaphore_signal(barrier, inc=1, device_id=peer, device_id_type=MESH)

    fetches = [
        (prev_hbm, prev), (hts_hbm, hts), (trn_hbm, trn), (v_hbm, v_rows), (u_hbm.at[dm], u_rows), (zin_hbm, zin),
        (aw_hbm, aw), (cell_hbm.at[dm], cell), (cnt_hbm, cnt), (nbr_hbm, nbr), (inc_hbm, inc),
    ]
    fetches = [pltpu.make_async_copy(a, b, csem.at[n]) for n, (a, b) in enumerate(fetches)]
    for fetch in fetches:
        fetch.start()

    wide = (RD, XD)
    lane16 = lanes_of(wide)
    small = (8, 128)
    lane8 = lanes_of(small)
    sub8 = rows_of(small)

    def pack_edges(parts, to_left, to_right):
        a = jnp.zeros(wide, f32)
        b = jnp.zeros(wide, f32)
        for c, part in enumerate(parts):
            here = lane16 // 8 == c
            a = jnp.where(here, part if c == 0 else pltpu.roll(part, 8 * c, 1), a)
            b = jnp.where(here, pltpu.roll(part, 8 * c + 3, 1), b)
        to_left[...] = a
        to_right[...] = b

    for fetch in fetches[:2]:
        fetch.wait()
    for c in range(4):
        cbuf[c, 8:24, :] = prev[c]
    cbuf[4, 8:24, :] = hts[...]
    pack_edges([prev[0], prev[1], prev[2], prev[3], hts[...]], pk_l, pk_r)
    zero8 = jnp.zeros(small, f32)
    li, lj = lane8 // 16, lane8 % 16
    for slot in (0, nd + 1):
        gr[slot] = zero8
        fr[slot] = jnp.zeros((4, 128), f32)
        tr[slot] = jnp.zeros((2, 128), f32)
    fetches[2].wait()
    row_buf[...] = zero8
    row_buf[4:6, 0:Q] = trn[0]
    share_rows = jnp.where(lj < 8, pick(row_buf[...], (li * 8 + lj) & 127), 0.0)
    share_msg[...] = share_rows[4:6, :]

    pl.semaphore_wait(barrier, nd - 1 + nx - 1 + 4)

    def halo(buf, e_l, e_r, p_l, p_r, send, recv):
        plan = [
            (p_l.at[0:8, :], e_r.at[24:32, :], (up, left)),
            (p_l.at[8:16, :], e_r.at[0:8, :], (down, left)),
            (p_r.at[0:8, :], e_l.at[24:32, :], (up, right)),
            (p_r.at[8:16, :], e_l.at[0:8, :], (down, right)),
            (buf.at[:, 8:16, :], buf.at[:, 24:32, :], (up, x)),
            (buf.at[:, 16:24, :], buf.at[:, 0:8, :], (down, x)),
            (p_l, e_r.at[8:24, :], (d, left)),
            (p_r, e_l.at[8:24, :], (d, right)),
        ]
        return [
            pltpu.make_async_remote_copy(
                src_ref=src, dst_ref=dst, send_sem=send.at[n], recv_sem=recv.at[n],
                device_id=dev, device_id_type=MESH,
            )
            for n, (src, dst, dev) in enumerate(plan)
        ]

    halo1 = halo(cbuf, edge_l, edge_r, pk_l, pk_r, hs_sem, hr_sem)
    for copy in halo1:
        copy.start()
    for to in blocks:
        pltpu.make_async_remote_copy(
            src_ref=share_msg, dst_ref=tr.at[d + 1], send_sem=trs, recv_sem=trr,
            device_id=(to, x), device_id_type=MESH,
        ).start()

    for fetch in fetches[3:6]:
        fetch.wait()
    power16 = (rows_of(wide) - 7).astype(f32) * 0.03

    def fill(r, carry):
        at = pl.ds(pl.multiple_of(r * XD, XD), XD)
        hrow = jnp.broadcast_to(hts[pl.ds(r, 1), :], wide)
        hs, hc = sincos_small(power16 * hrow)
        vc0, vs0 = v_rows[0], v_rows[1]
        vc = hc * vc0 - hs * vs0
        vs = hc * vs0 + hs * vc0
        tab_v[0, :, at] = vc[:8]
        tab_v[1, :, at] = vs[:8]
        c8, s8 = squared(*squared(*squared(hc, hs)))
        pc, ps = u_rows[r, 0], u_rows[r, 1]
        cc_, ss_, cs_, sc_ = c8 * pc, s8 * ps, c8 * ps, s8 * pc
        for n, value in enumerate((cc_ - ss_, sc_ + cs_, cc_ + ss_, sc_ - cs_)):
            high, low = split(value)
            tab_u_h[16 * n : 16 * n + 16, at] = high
            tab_u_l[16 * n : 16 * n + 16, at] = low
        for f in range(F):
            zr = jnp.broadcast_to(zin[2 * f, pl.ds(r, 1), :], wide)
            zi = jnp.broadcast_to(zin[2 * f + 1, pl.ds(r, 1), :], wide)
            for n, value in enumerate((zr * vc - zi * vs, zr * vs + zi * vc)):
                high, low = split(value)
                k = 2 * f + n
                tab_a_h[16 * k : 16 * k + 16, at] = high
                tab_a_l[16 * k : 16 * k + 16, at] = low
        return carry

    lax.fori_loop(0, RD, fill, 0)

    y = contract3(tab_u_h[...], tab_u_l[...], tab_a_h[...], tab_a_l[...])
    yc = jnp.concatenate([y[0:16], y[32:48]], axis=1)
    ys = jnp.concatenate([y[16:32], y[48:64]], axis=1)
    gx[x] = yc + jnp.where((lane16 // 16) % 2 == 0, -pltpu.roll(ys, 112, 1), pltpu.roll(ys, 16, 1))

    def spread_xr(buf, send, recv):
        for to in owners:
            pltpu.make_async_remote_copy(
                src_ref=buf.at[x], dst_ref=buf.at[x], send_sem=send, recv_sem=recv,
                device_id=(d, to), device_id_type=MESH,
            ).start()

    def await_bytes(view, sem):
        pltpu.make_async_copy(view, view, sem).wait()

    def total_xr(buf):
        total = buf[0]
        for k in range(1, nx):
            total = total + buf[k]
        return total

    spread_xr(gx, gxs, gxr)

    for fetch in fetches[6:]:
        fetch.wait()
    for f in range(F):
        for c in range(2):
            row_buf[2 * f + c : 2 * f + c + 1, 0:Q] = aw[f, c : c + 1, :]
    weight_rows = [jnp.broadcast_to(row_buf[k : k + 1, :], small) * spread for k in range(4)]
    for k in range(4):
        w_lane[k] = jnp.where(lj < 8, pick(weight_rows[k], (li * 8 + lj) & 127), 0.0)
    for i in range(8):
        for k in range(4):
            w_sub[k, i] = pick(weight_rows[k], sub8 + 8 * i)

    hh = hts[...]
    hs, hc = sincos_small(0.03 * hh)
    c8, s8 = squared(*squared(*squared(hc, hs)))
    vu[0] = hc * cell[10] - hs * cell[11]
    vu[1] = hc * cell[11] + hs * cell[10]
    vu[2] = c8 * cell[8] - s8 * cell[9]
    vu[3] = s8 * cell[8] + c8 * cell[9]
    vu[4] = c8 * cell[8] + s8 * cell[9]
    vu[5] = s8 * cell[8] - c8 * cell[9]
    for f in range(F):
        s, c = sincos((0.3 + 0.2 * f) * hh)
        for way in range(2):
            k = way * 4 + f * 2
            base[k] = c * cell[k] - s * cell[k + 1]
            base[k + 1] = s * cell[k] + c * cell[k + 1]

    def note(l, words):
        word0, word1 = words
        code = nbr[l]
        m = jnp.where(code >= 24, code + 1, code)
        low = m < 28
        bit = jnp.where(l < cnt[...], jnp.left_shift(1, jnp.where(low, m, m - 28)), 0)
        return word0 | jnp.where(low, bit, 0), word1 | jnp.where(low, 0, bit)

    zero_word = jnp.zeros(wide, i32)
    words = lax.fori_loop(0, LMAX, note, (zero_word, zero_word))

    tall = (32, XD)
    lane32 = lanes_of(tall)
    row32 = rows_of(tall) + (d * RD - 8)
    inside = (row32 >= 0) & (row32 < nd * RD)

    def shift_all(buf, e_l, e_r, count):
        el = jnp.where(inside & (lane32 < 128 * x), e_l[...], 0.0)
        er = jnp.where(inside & (lane32 < 128 * (nx - 1 - x)), e_r[...], 0.0)
        for c in range(count):
            mid = jnp.where(inside, buf[c], 0.0)
            shifted[H, c] = mid
            for k in range(1, H + 1):
                shifted[H + k, c] = jnp.where(
                    lane32 >= 128 - k,
                    pltpu.roll(er, (128 - k - 8 * c) % 128, 1),
                    pltpu.roll(mid, 128 - k, 1),
                )
                shifted[H - k, c] = jnp.where(
                    lane32 < k,
                    pltpu.roll(el, (k - 3 - 8 * c) % 128, 1),
                    pltpu.roll(mid, k, 1),
                )

    def window(dyi, c, dx):
        return shifted[dyi, c, 8 + dx : 24 + dx, :]

    def applied(total, g, dyi, dx):
        out = []
        for f in range(F):
            gr_, gi_ = g[2 * f], g[2 * f + 1]
            ur, ui = window(dyi, 2 * f, dx), window(dyi, 2 * f + 1, dx)
            out.append(total[2 * f] + (gr_ * ur - gi_ * ui))
            out.append(total[2 * f + 1] + (gr_ * ui + gi_ * ur))
        return tuple(out)

    for copy in halo1:
        copy.wait_recv()
    shift_all(cbuf, edge_l, edge_r, 5)

    def couple(dyi, total):
        dy = dyi - H
        for dxi in range(SIDE):
            dx = dxi - H
            square = jnp.maximum(dx * dx + dy * dy, 1).astype(f32)
            rise = window(dyi, 4, dx) - hh
            dist2 = square + rise * rise
            inv = lax.rsqrt(dist2)
            inv = inv * (1.5 - 0.5 * dist2 * (inv * inv))
            bits = words[dxi // 4] >> (7 * (dxi % 4) + dyi)
            mag = jnp.where((bits & 1) == 1, 0.25 * inv, 0.0)
            s1, c1 = sincos((math.pi / 8) * (dist2 * inv) - 0.5 * math.pi)
            s1, c1 = c1, -s1
            c4, s4 = squared(*squared(c1, s1))
            g = (
                mag * c4,
                mag * s4,
                mag * (c4 * c1 - s4 * s1),
                mag * (s4 * c1 + c4 * s1),
            )
            for c in range(4):
                table[dyi, dxi, c] = g[c]
            total = applied(total, g, dyi, dx)
        return total

    def recouple(dyi, total):
        for dxi in range(SIDE):
            g = [table[dyi, dxi, c] for c in range(4)]
            total = applied(total, g, dyi, dxi - H)
        return total

    nothing = (jnp.zeros(wide, f32),) * 4
    near_old = lax.fori_loop(0, SIDE, couple, nothing)

    def times_z(f, real, imag):
        zr, zi = zin[2 * f], zin[2 * f + 1]
        return zr * real - zi * imag, zr * imag + zi * real

    def project(way, field, buf, send, recv):
        lj_even = (lane8 // 8) % 2 == 0
        for f in range(F):
            k = way * 4 + f * 2
            br, bi = base[k], base[k + 1]
            sr, si = field[2 * f], field[2 * f + 1]
            srcp[2 * f] = br * sr + bi * si
            srcp[2 * f + 1] = br * si - bi * sr

        def lay(r, carry):
            at = pl.ds(pl.multiple_of(r * XD, XD), XD)
            vc, vs = tab_v[0, :, at], tab_v[1, :, at]
            for f in range(F):
                sr = jnp.broadcast_to(srcp[2 * f, pl.ds(r, 1), :], small)
                si = jnp.broadcast_to(srcp[2 * f + 1, pl.ds(r, 1), :], small)
                both = jnp.concatenate([sr * vc - si * vs, sr * vs + si * vc], axis=0)
                high, low = split(both)
                tab_f_h[16 * f : 16 * f + 16, at] = high
                tab_f_l[16 * f : 16 * f + 16, at] = low
            return carry

        lax.fori_loop(0, RD, lay, 0)
        rows = slice(32 * way, 32 * way + 32)
        y = contract3(tab_u_h[rows, :], tab_u_l[rows, :], tab_f_h[...], tab_f_l[...])
        pad = jnp.zeros((8, 96), f32)
        yc = jnp.concatenate([y[0:8], pad], axis=1)
        ys = jnp.concatenate([y[16:24], pad], axis=1)
        sums = yc + jnp.where(lj_even, -pltpu.roll(ys, 120, 1), pltpu.roll(ys, 8, 1))
        for k in range(4):
            row = pick(sums, 8 * k + 7 - (lj & 7))
            row = jnp.where(sub8 == 7 - li, row, 0.0)
            buf[x, k : k + 1, :] = jnp.sum(row, axis=0, keepdims=True)
        spread_xr(buf, send, recv)

    for f in range(F):
        sr, si = times_z(f, inc[2 * f] - near_old[2 * f], inc[2 * f + 1] - near_old[2 * f + 1])
        loaded[2 * f] = sr
        loaded[2 * f + 1] = si
    project(0, loaded, fx, fxs, fxr)

    await_bytes(gx.at[pl.ds(0, nx - 1)], gxr)
    g_sum = total_xr(gx)
    h0, h1 = regroup(g_sum[:8]), regroup(g_sum[8:])
    gmsg[0] = jnp.where(sub8 < 4, h0, pltpu.roll(h1, 4, 0))
    gmsg[1] = jnp.where(sub8 < 4, pltpu.roll(h0, 4, 0), h1)

    for to in blocks:
        pltpu.make_async_remote_copy(
            src_ref=gmsg.at[(to < d).astype(i32)], dst_ref=gr.at[d + 1],
            send_sem=grs, recv_sem=grr.at[d],
            device_id=(to, x), device_id_type=MESH,
        ).start()

    def send_feed(way, buf, recv, msg):
        await_bytes(buf.at[pl.ds(0, nx - 1)], recv)
        msg[...] = total_xr(buf)
        for to in blocks:

            @pl.when(to < d if way else to > d)
            def _():
                pltpu.make_async_remote_copy(
                    src_ref=msg, dst_ref=fr.at[d + 1], send_sem=frs, recv_sem=frr.at[d],
                    device_id=(to, x), device_id_type=MESH,
                ).start()

    def await_slots(buf, sem, first, last):
        def step(k, carry):
            await_bytes(buf.at[k + 1], sem.at[k])
            return carry

        lax.fori_loop(first, last, step, 0)

    def build(slot, first):
        if first:
            start = (7 - li) * 16 + sub8 - lj + 7
        else:
            start = (li + 7) * 16 + lj - sub8 + 7
        g = [
            [jnp.broadcast_to(gr[slot, r : r + 1, :], small) for r in (k, 4 + k)]
            for k in range(4)
        ]
        if not first:
            index = (lane8 & 7) * 16 + sub8
            shares = [pick(jnp.broadcast_to(tr[slot, f : f + 1, :], small), index) for f in range(F)]
            shares = jnp.where(lane8 < 8, shares[0], shares[1])
        for i in range(8):
            src = start + 16 * i if first else start - 16 * i
            index = src & 127
            near = src < 128
            m = [jnp.where(near, pick(g[k][0], index), pick(g[k][1], index)) for k in range(4)]
            own = lane8 == sub8 + 16 * i
            if not first:
                own = own | (lane8 == sub8 + (16 * i + 8))
            for f in range(F):
                mr, mi = m[2 * f], m[2 * f + 1]
                if first:
                    wr, wi = w_sub[2 * f, i], w_sub[2 * f + 1, i]
                else:
                    wr, wi = w_lane[2 * f], w_lane[2 * f + 1]
                real = jnp.where(own, 1.0, 0.0) - (mr * wr - mi * wi)
                imag = -(mr * wi + mi * wr)
                if not first:
                    at = 8 * f + i
                    share = jnp.broadcast_to(shares[:, at : at + 1], small)
                    real, imag = share * real, share * imag
                mats[slot, f, 0, i] = real
                mats[slot, f, 1, i] = imag

    def slots_of(way, t):
        if way == 0:
            at = 2 * t - lax.rem(d, 2)
            return at + 1, at + 2
        at = 2 * t - lax.rem(nd - 1 - d, 2)
        return nd - at, nd - at - 1

    def pairs_of(way):
        return (d + 1) // 2 if way == 0 else (nd - d) // 2

    def await_blocks(way, buf, sem):
        if way == 0:
            await_slots(buf, sem, 0, d)
        else:
            await_slots(buf, sem, d + 1, nd)

    def build_all(way):
        def step(t, carry):
            one, two = slots_of(way, t)
            build(one, True)
            build(two, False)
            return carry

        lax.fori_loop(0, pairs_of(way), step, 0)

    def sweep(way):
        for f in range(F):
            for c in range(2):
                for i in range(8):
                    state[f, c, i] = zero8

        def tree(terms):
            while len(terms) > 1:
                terms = [a + b for a, b in zip(terms[::2], terms[1::2])]
            return terms[0]

        def step(t, carry):
            one, two = slots_of(way, t)
            for f in range(F):
                tr_, ti_ = [], []
                for i in range(8):
                    mr, mi = mats[one, f, 0, i], mats[one, f, 1, i]
                    sr, si = state[f, 0, i], state[f, 1, i]
                    tr_.append(mr * sr - mi * si)
                    ti_.append(mr * si + mi * sr)
                share = tr[one, f : f + 1, :]
                y = []
                for c, terms in enumerate((tr_, ti_)):
                    k = 2 * f + c
                    row = share * (jnp.sum(tree(terms), axis=0, keepdims=True) + fr[one, k : k + 1, :])
                    row = row + jnp.where(lj[:1] < 8, 0.0, fr[two, k : k + 1, :])
                    y.append(jnp.broadcast_to(row, small))
                yr, yi = y
                for i in range(8):
                    mr, mi = mats[two, f, 0, i], mats[two, f, 1, i]
                    vr = jnp.sum(mr * yr - mi * yi, axis=1, keepdims=True)
                    vi = jnp.sum(mr * yi + mi * yr, axis=1, keepdims=True)
                    state[f, 0, i] = jnp.broadcast_to(vr, small)
                    state[f, 1, i] = jnp.broadcast_to(vi, small)
            return carry

        lax.fori_loop(0, pairs_of(way), step, 0)

    def radiate(way):
        for f in range(F):
            for i in range(8):
                wr, wi = w_sub[2 * f, i], w_sub[2 * f + 1, i]
                sr, si = state[f, 0, i], state[f, 1, i]
                state[f, 0, i] = wr * sr - wi * si
                state[f, 1, i] = wr * si + wi * sr
        vr, vi = vu[0], vu[1]
        ur, ui = vu[2 + 2 * way], vu[3 + 2 * way]

        def step(n, total):
            i = 7 - n
            out = []
            for f in range(F):
                tr, ti = total[2 * f], total[2 * f + 1]

                def coef(c, j):
                    return jnp.broadcast_to(state[f, c, i, j : j + 1, :], wide)

                ar, ai = coef(0, 7), coef(1, 7)
                for j in range(6, -1, -1):
                    ar, ai = ar * vr - ai * vi + coef(0, j), ar * vi + ai * vr + coef(1, j)
                out += [tr * ur - ti * ui + ar, tr * ui + ti * ur + ai]
            return tuple(out)

        total = lax.fori_loop(0, 8, step, nothing)
        out = []
        for f in range(F):
            k = way * 4 + f * 2
            br, bi = base[k], base[k + 1]
            tr, ti = total[2 * f], total[2 * f + 1]
            out += [br * tr - bi * ti, br * ti + bi * tr]
        return out

    send_feed(0, fx, fxr, fmsg)
    await_bytes(tr.at[pl.ds(0, nd - 1)], trr)
    await_blocks(0, gr, grr)
    build_all(0)
    await_blocks(0, fr, frr)
    sweep(0)
    weak = radiate(0)
    flow = []
    for f in range(F):
        ar, ai = times_z(f, weak[2 * f], weak[2 * f + 1])
        flow += [loaded[2 * f] - ar, loaded[2 * f + 1] - ai]
    for c in range(4):
        out_f[c] = flow[c]
        cbuf2[c, 8:24, :] = flow[c]
        weakf[c] = weak[c]
    pack_edges(flow, pk_l2, pk_r2)
    halo2 = halo(cbuf2, edge_l2, edge_r2, pk_l2, pk_r2, hs2_sem, hr2_sem)
    for copy in halo2:
        copy.start()

    await_blocks(1, gr, grr)
    build_all(1)
    for copy in halo2:
        copy.wait_recv()
    shift_all(cbuf2, edge_l2, edge_r2, 4)
    near_new = lax.fori_loop(0, SIDE, recouple, nothing)
    for f in range(F):
        dr, di = times_z(
            f,
            inc[2 * f] - near_new[2 * f] - weakf[2 * f],
            inc[2 * f + 1] - near_new[2 * f + 1] - weakf[2 * f + 1],
        )
        driven[2 * f] = dr
        driven[2 * f + 1] = di
    project(1, driven, fx2, fxs2, fxr2)
    send_feed(1, fx2, fxr2, fmsg2)
    await_blocks(1, fr, frr)
    sweep(1)
    weak = radiate(1)
    for f in range(F):
        ar, ai = times_z(f, weak[2 * f], weak[2 * f + 1])
        out_c[2 * f] = driven[2 * f] - ar
        out_c[2 * f + 1] = driven[2 * f + 1] - ai

    for copy in halo1 + halo2:
        copy.wait_send()
    await_bytes(gx.at[pl.ds(0, nx - 1)], gxs)
    await_bytes(fx.at[pl.ds(0, nx - 1)], fxs)
    await_bytes(fx2.at[pl.ds(0, nx - 1)], fxs2)
    await_bytes(gr.at[pl.ds(0, nd - 1)], grs)
    await_bytes(fr.at[pl.ds(0, nd - 1)], frs)
    await_bytes(tr.at[pl.ds(0, nd - 1)], trs)


def solution(mesh):
    nd, nx = mesh.shape["rng"], mesh.shape["xr"]
    v_rows, u_rows, cell = phase_tables()

    def per_device(incident, inverse_diag, previous, heights, neighbours, counts, transmit, angle_weights):
        vmem = pl.BlockSpec(memory_space=pltpu.VMEM)
        far = pl.BlockSpec(memory_space=pltpu.HBM)
        points = RD * XD
        block = jax.ShapeDtypeStruct((2 * F, RD, XD), f32)
        V = pltpu.VMEM
        dma = pltpu.SemaphoreType.DMA
        held = [V(a.shape, a.dtype) for a in (
            incident, inverse_diag, previous, heights, neighbours, counts, transmit, angle_weights, v_rows
        )]
        scratch = held + [
            V((RD, 2, 16, XD), f32), V((12, RD, XD), f32),
            V((5, 32, XD), f32), V((32, XD), f32), V((32, XD), f32), V((RD, XD), f32), V((RD, XD), f32),
            V((4, 32, XD), f32), V((32, XD), f32), V((32, XD), f32), V((RD, XD), f32), V((RD, XD), f32),
            V((SIDE, 5, 32, XD), f32), V((SIDE, SIDE, 4, RD, XD), f32),
            V((64, points), bf16), V((64, points), bf16), V((64, points), bf16), V((64, points), bf16),
            V((2, 8, points), f32), V((32, points), bf16), V((32, points), bf16),
            V((4, RD, XD), f32), V((4, RD, XD), f32), V((4, RD, XD), f32), V((4, RD, XD), f32),
            V((4, 8, 128), f32), V((4, 8, 8, 128), f32), V((8, 128), f32), V((2, 128), f32), V((nd + 2, 2, 128), f32),
            V((nx, 16, 128), f32), V((2, 8, 128), f32), V((nd + 2, 8, 128), f32),
            V((nx, 4, 128), f32), V((nx, 4, 128), f32), V((4, 128), f32), V((4, 128), f32),
            V((nd + 2, 4, 128), f32), V((nd + 2, F, 2, 8, 8, 128), f32), V((F, 2, 8, 8, 128), f32),
            V((8, RD, XD), f32), V((6, RD, XD), f32),
            dma((11,)), dma((8,)), dma((8,)), dma((8,)), dma((8,)),
            dma, dma, dma, dma((nd,)), dma, dma, dma, dma, dma, dma((nd,)), dma, dma,
        ]
        return pl.pallas_call(
            functools.partial(kernel, nd, nx),
            out_shape=(block, block),
            in_specs=[far] * 11,
            out_specs=(vmem, vmem),
            scratch_shapes=scratch,
            compiler_params=pltpu.CompilerParams(
                collective_id=0, has_side_effects=True, vmem_limit_bytes=60 << 20
            ),
        )(
            incident, inverse_diag, previous, heights, neighbours, counts, transmit, angle_weights,
            jnp.asarray(v_rows), jnp.asarray(u_rows), jnp.asarray(cell),
        )

    placed = (
        P(None, "rng", "xr"),
        P(None, "rng", "xr"),
        P(None, "rng", "xr"),
        P("rng", "xr"),
        P(None, "rng", "xr"),
        P("rng", "xr"),
        P("rng", None, None),
        P(),
    )
    return jax.shard_map(
        per_device,
        mesh=mesh,
        in_specs=placed,
        out_specs=(P(None, "rng", "xr"), P(None, "rng", "xr")),
        check_vma=False,
    )
```

```python
import functools
import math

import jax
import jax.numpy as jnp
import numpy as np
from jax import lax
from jax.experimental import pallas as pl
from jax.experimental.pallas import tpu as pltpu
from jax.sharding import PartitionSpec as P

F = 2
Q = 64
H = 3
LMAX = 24
RD = 16
XD = 128
SIDE = 2 * H + 1
MESH = pl.DeviceIdType.MESH
f32 = jnp.float32
bf16 = jnp.bfloat16
i32 = jnp.int32


def phase_tables():
    turn = 2.0 * math.pi / 64
    power = np.arange(16) - 7
    cols = np.arange(XD)
    ang = turn * ((power[:, None] * cols[None, :]) % 64)
    v_rows = np.stack([np.cos(ang), np.sin(ang)]).astype(np.float32)
    u_rows = np.zeros((4, RD, 2, 16, XD), np.float32)
    cell = np.zeros((4, 12, RD, XD), np.float32)
    for dm in range(4):
        rows = 16 * dm + np.arange(RD)
        ang = turn * ((power[None, :] * rows[:, None]) % 64)
        u_rows[dm, :, 0] = np.cos(ang)[:, :, None]
        u_rows[dm, :, 1] = np.sin(ang)[:, :, None]
        for way, sign in enumerate((1, -1)):
            for f in range(F):
                ang = turn * ((sign * (1 + 2 * f) * rows[:, None] + (f - 4) * cols[None, :]) % 64)
                cell[dm, way * 4 + f * 2] = np.cos(ang)
                cell[dm, way * 4 + f * 2 + 1] = np.sin(ang)
        ang = turn * ((rows[:, None] + 0 * cols[None, :]) % 64)
        cell[dm, 8], cell[dm, 9] = np.cos(ang), np.sin(ang)
        ang = turn * ((0 * rows[:, None] + cols[None, :]) % 64)
        cell[dm, 10], cell[dm, 11] = np.cos(ang), np.sin(ang)
    lane = np.arange(XD)
    side = np.where(lane < 8, lane - 3, lane + 120)
    wide = np.zeros((4, 8, 4, RD, XD), np.float32)
    for dm in range(4):
        rows = 16 * dm - 8 + np.arange(32)
        row_at = np.stack([np.r_[rows[:8], rows[:8]], rows[8:24], rows[8:24], np.r_[rows[24:], rows[24:]]])
        half = np.concatenate([np.tile(lane, (8, 1)), np.tile(side, (8, 1))])
        col_at = np.stack([half, np.tile(lane, (RD, 1)), np.tile(side, (RD, 1)), half])
        row_at = row_at[:, :, None] + 0 * col_at
        angs = [(1 + 2 * f) * row_at + (f - 4) * col_at for f in range(F)] + [row_at, col_at]
        for n, ang in enumerate(angs):
            wide[dm, 2 * n] = np.cos(turn * (ang % 64))
            wide[dm, 2 * n + 1] = np.sin(turn * (ang % 64))
    return v_rows, u_rows, cell, wide


def sincos_small(t):
    q = t * t
    s = t * (1.0 + q * (-1.0 / 6 + q * (1.0 / 120 + q * (-1.0 / 5040 + q * (1.0 / 362880)))))
    c = 1.0 + q * (-0.5 + q * (1.0 / 24 + q * (-1.0 / 720 + q * (1.0 / 40320))))
    return s, c


def sincos(t):
    q = t * t
    s = t * (
        1.0
        + q
        * (
            -1.0 / 6
            + q * (1.0 / 120 + q * (-1.0 / 5040 + q * (1.0 / 362880 + q * (-1.0 / 39916800))))
        )
    )
    c = 1.0 + q * (
        -0.5
        + q
        * (
            1.0 / 24
            + q
            * (-1.0 / 720 + q * (1.0 / 40320 + q * (-1.0 / 3628800 + q * (1.0 / 479001600))))
        )
    )
    return s, c


def squared(c, s):
    return c * c - s * s, 2.0 * (c * s)


def lanes_of(shape):
    return lax.broadcasted_iota(i32, shape, 1)


def rows_of(shape):
    return lax.broadcasted_iota(i32, shape, 0)


def pick(value, index):
    return jnp.take_along_axis(value, index, axis=1, mode="promise_in_bounds")


def split(value):
    high = value.astype(bf16)
    return high, (value - high.astype(f32)).astype(bf16)


def contract(left, right):
    return lax.dot_general(left, right, (((1,), (1,)), ((), ())), preferred_element_type=f32)


def contract3(left_high, left_low, right_high, right_low):
    return (
        contract(left_high, right_high)
        + contract(left_high, right_low)
        + contract(left_low, right_high)
    )


def regroup(value):
    shape = (8, 128)
    part = (rows_of(shape) - lanes_of(shape) // 16) & 7
    out = jnp.zeros(shape, f32)
    for s in range(8):
        moved = value
        if s:
            moved = pltpu.roll(pltpu.roll(value, 128 - 16 * s, 1), s, 0)
        out = jnp.where(part == s, moved, out)
    return out


def kernel(
    nd, nx,
    inc_hbm, zin_hbm, prev_hbm, hts_hbm, nbr_hbm, cnt_hbm, trn_hbm, aw_hbm, v_hbm, u_hbm, cell_hbm, wide_hbm,
    out_f, out_c,
    inc, zin, prev, hts, nbr, cnt, trn, aw, v_rows, u_rows, cell, wide_cell, pz, psrc, pwave, cflow, eflow, near_rows, cbuf, edge_l, edge_r, pk_l, pk_r,
    cbuf2, edge_l2, edge_r2, pk_l2, pk_r2,
    shifted, table, tab_u_h, tab_u_l, tab_a_h, tab_a_l, tab_v, tab_f_h, tab_f_l,
    srcp, loaded, driven, weakf, w_lane, w_sub, row_buf, share_msg, tr,
    gx, gmsg, gr, fx, fx2, fmsg, fmsg2, fr, mats, state,
    base, vu,
    csem, hs_sem, hr_sem, hs2_sem, hr2_sem,
    gxs, gxr, grs, grr, fxs, fxr, fxs2, fxr2, frs, frr, trs, trr,
):
    d = lax.axis_index("rng")
    x = lax.axis_index("xr")
    dm = lax.rem(d, 4)
    spread = 1.0 / math.sqrt(RD * XD * nx)
    up, down = lax.rem(d + nd - 1, nd), lax.rem(d + 1, nd)
    left, right = lax.rem(x + nx - 1, nx), lax.rem(x + 1, nx)

    def turned(value, by, size):
        moved = value + by
        return jnp.where(moved >= size, moved - size, moved)

    nc = min(4, nd)
    nr = nd // nc
    far = lambda n, size: min(n, size - n)
    others = sorted(
        ((a, b) for a in range(nr) for b in range(nc) if a or b),
        key=lambda p: -far(p[0], nr) - far(p[1], nc),
    )
    d_row, d_col = d // nc, lax.rem(d, nc)
    blocks = [turned(d_row, a, nr) * nc + turned(d_col, b, nc) for a, b in others]
    owners = [turned(x, n, nx) for n in sorted(range(1, nx), key=lambda n: -far(n, nx))]

    barrier = pltpu.get_barrier_semaphore()
    peers = [(to, x) for to in blocks] + [(d, to) for to in owners]
    peers += [(dd, xx) for dd in (up, down) for xx in (left, right)]
    for peer in peers:
        pl.semaphore_signal(barrier, inc=1, device_id=peer, device_id_type=MESH)

    fetches = [
        (prev_hbm, prev), (hts_hbm, hts), (zin_hbm, zin), (trn_hbm, trn), (v_hbm, v_rows), (u_hbm.at[dm], u_rows),
        (aw_hbm, aw), (cell_hbm.at[dm], cell), (cnt_hbm, cnt), (nbr_hbm, nbr), (inc_hbm, inc),
        (wide_hbm.at[dm], wide_cell),
    ]
    fetches = [pltpu.make_async_copy(a, b, csem.at[n]) for n, (a, b) in enumerate(fetches)]
    for fetch in fetches:
        fetch.start()

    wide = (RD, XD)
    lane16 = lanes_of(wide)
    small = (8, 128)
    lane8 = lanes_of(small)
    sub8 = rows_of(small)

    def pack_edges(parts, to_left, to_right):
        a = jnp.zeros(wide, f32)
        b = jnp.zeros(wide, f32)
        for c, part in enumerate(parts):
            here = lane16 // 8 == c
            a = jnp.where(here, part if c == 0 else pltpu.roll(part, 8 * c, 1), a)
            b = jnp.where(here, pltpu.roll(part, 8 * c + 3, 1), b)
        to_left[...] = a
        to_right[...] = b

    for fetch in fetches[:3]:
        fetch.wait()
    for c in range(4):
        cbuf[c, 8:24, :] = prev[c]
        cbuf[5 + c, 8:24, :] = zin[c]
    cbuf[4, 8:24, :] = hts[...]
    pack_edges([prev[c] for c in range(4)] + [hts[...]] + [zin[c] for c in range(4)], pk_l, pk_r)
    zero8 = jnp.zeros(small, f32)
    li, lj = lane8 // 16, lane8 % 16
    for slot in (0, nd + 1):
        gr[slot] = zero8
        fr[slot] = jnp.zeros((4, 128), f32)
        tr[slot] = jnp.zeros((2, 128), f32)
    fetches[3].wait()
    row_buf[...] = zero8
    row_buf[4:6, 0:Q] = trn[0]
    share_rows = jnp.where(lj < 8, pick(row_buf[...], (li * 8 + lj) & 127), 0.0)
    share_msg[...] = share_rows[4:6, :]
    tr[d + 1] = share_rows[4:6, :]

    pl.semaphore_wait(barrier, nd - 1 + nx - 1 + 4)

    def halo(buf, e_l, e_r, p_l, p_r, send, recv):
        plan = [
            (p_l.at[0:8, :], e_r.at[24:32, :], (up, left)),
            (p_l.at[8:16, :], e_r.at[0:8, :], (down, left)),
            (p_r.at[0:8, :], e_l.at[24:32, :], (up, right)),
            (p_r.at[8:16, :], e_l.at[0:8, :], (down, right)),
            (buf.at[:, 8:16, :], buf.at[:, 24:32, :], (up, x)),
            (buf.at[:, 16:24, :], buf.at[:, 0:8, :], (down, x)),
            (p_l, e_r.at[8:24, :], (d, left)),
            (p_r, e_l.at[8:24, :], (d, right)),
        ]
        return [
            pltpu.make_async_remote_copy(
                src_ref=src, dst_ref=dst, send_sem=send.at[n], recv_sem=recv.at[n],
                device_id=dev, device_id_type=MESH,
            )
            for n, (src, dst, dev) in enumerate(plan)
        ]

    halo1 = halo(cbuf, edge_l, edge_r, pk_l, pk_r, hs_sem, hr_sem)
    for copy in halo1:
        copy.start()
    for to in blocks:
        pltpu.make_async_remote_copy(
            src_ref=share_msg, dst_ref=tr.at[d + 1], send_sem=trs, recv_sem=trr,
            device_id=(to, x), device_id_type=MESH,
        ).start()

    for fetch in fetches[4:6]:
        fetch.wait()
    power16 = (rows_of(wide) - 7).astype(f32) * 0.03

    def fill(r, carry):
        at = pl.ds(pl.multiple_of(r * XD, XD), XD)
        hrow = jnp.broadcast_to(hts[pl.ds(r, 1), :], wide)
        hs, hc = sincos_small(power16 * hrow)
        vc0, vs0 = v_rows[0], v_rows[1]
        vc = hc * vc0 - hs * vs0
        vs = hc * vs0 + hs * vc0
        tab_v[0, :, at] = vc[:8]
        tab_v[1, :, at] = vs[:8]
        c8, s8 = squared(*squared(*squared(hc, hs)))
        pc, ps = u_rows[r, 0], u_rows[r, 1]
        cc_, ss_, cs_, sc_ = c8 * pc, s8 * ps, c8 * ps, s8 * pc
        for n, value in enumerate((cc_ - ss_, sc_ + cs_, cc_ + ss_, sc_ - cs_)):
            high, low = split(value)
            tab_u_h[16 * n : 16 * n + 16, at] = high
            tab_u_l[16 * n : 16 * n + 16, at] = low
        for f in range(F):
            zr = jnp.broadcast_to(zin[2 * f, pl.ds(r, 1), :], wide)
            zi = jnp.broadcast_to(zin[2 * f + 1, pl.ds(r, 1), :], wide)
            for n, value in enumerate((zr * vc - zi * vs, zr * vs + zi * vc)):
                high, low = split(value)
                k = 2 * f + n
                tab_a_h[16 * k : 16 * k + 16, at] = high
                tab_a_l[16 * k : 16 * k + 16, at] = low
        return carry

    lax.fori_loop(0, RD, fill, 0)

    y = contract3(tab_u_h[...], tab_u_l[...], tab_a_h[...], tab_a_l[...])
    yc = jnp.concatenate([y[0:16], y[32:48]], axis=1)
    ys = jnp.concatenate([y[16:32], y[48:64]], axis=1)
    gx[x] = yc + jnp.where((lane16 // 16) % 2 == 0, -pltpu.roll(ys, 112, 1), pltpu.roll(ys, 16, 1))

    def spread_xr(buf, send, recv):
        for to in owners:
            pltpu.make_async_remote_copy(
                src_ref=buf.at[x], dst_ref=buf.at[x], send_sem=send, recv_sem=recv,
                device_id=(d, to), device_id_type=MESH,
            ).start()

    def await_bytes(view, sem):
        pltpu.make_async_copy(view, view, sem).wait()

    def total_xr(buf):
        total = buf[0]
        for k in range(1, nx):
            total = total + buf[k]
        return total

    spread_xr(gx, gxs, gxr)

    for fetch in fetches[6:]:
        fetch.wait()
    for f in range(F):
        for c in range(2):
            row_buf[2 * f + c : 2 * f + c + 1, 0:Q] = aw[f, c : c + 1, :]
    weight_rows = [jnp.broadcast_to(row_buf[k : k + 1, :], small) * spread for k in range(4)]
    for k in range(4):
        w_lane[k] = jnp.where(lj < 8, pick(weight_rows[k], (li * 8 + lj) & 127), 0.0)
    for i in range(8):
        for k in range(4):
            w_sub[k, i] = pick(weight_rows[k], sub8 + 8 * i)

    hh = hts[...]
    hs, hc = sincos_small(0.03 * hh)
    c8, s8 = squared(*squared(*squared(hc, hs)))
    vu[0] = hc * cell[10] - hs * cell[11]
    vu[1] = hc * cell[11] + hs * cell[10]
    vu[2] = c8 * cell[8] - s8 * cell[9]
    vu[3] = s8 * cell[8] + c8 * cell[9]
    vu[4] = c8 * cell[8] + s8 * cell[9]
    vu[5] = s8 * cell[8] - c8 * cell[9]
    for f in range(F):
        s, c = sincos((0.3 + 0.2 * f) * hh)
        for way in range(2):
            k = way * 4 + f * 2
            base[k] = c * cell[k] - s * cell[k + 1]
            base[k + 1] = s * cell[k] + c * cell[k + 1]

    def note(l, words):
        word0, word1 = words
        code = nbr[l]
        m = jnp.where(code >= 24, code + 1, code)
        low = m < 28
        bit = jnp.where(l < cnt[...], jnp.left_shift(1, jnp.where(low, m, m - 28)), 0)
        return word0 | jnp.where(low, bit, 0), word1 | jnp.where(low, 0, bit)

    zero_word = jnp.zeros(wide, i32)
    words = lax.fori_loop(0, LMAX, note, (zero_word, zero_word))

    tall = (32, XD)
    lane32 = lanes_of(tall)
    row32 = rows_of(tall) + (d * RD - 8)
    inside = (row32 >= 0) & (row32 < nd * RD)

    def shift_all(buf, edges, count):
        to_left = inside & (lane32 < 128 * x)
        to_right = inside & (lane32 < 128 * (nx - 1 - x))
        for c in range(count):
            el, left_at, er, right_at = edges(c)
            el = jnp.where(to_left, el, 0.0)
            er = jnp.where(to_right, er, 0.0)
            mid = jnp.where(inside, buf[c], 0.0)
            shifted[H, c] = mid
            for k in range(1, H + 1):
                shifted[H + k, c] = jnp.where(
                    lane32 >= 128 - k,
                    pltpu.roll(er, (128 - k - right_at) % 128, 1),
                    pltpu.roll(mid, 128 - k, 1),
                )
                shifted[H - k, c] = jnp.where(
                    lane32 < k,
                    pltpu.roll(el, (k - 3 - left_at) % 128, 1),
                    pltpu.roll(mid, k, 1),
                )

    def sides(e_l, e_r, c):
        left_part = e_l[...] if c == 0 else pltpu.roll(e_l[...], 128 - 8 * c, 1)
        right_part = e_r[...] if c == 1 else pltpu.roll(e_r[...], (136 - 8 * c) % 128, 1)
        return jnp.where(lane32 < 8, left_part, right_part)

    def grouped(center, edge):
        return (
            jnp.concatenate([center[:8], edge[:8]], axis=0),
            center[8:24],
            edge[8:24],
            jnp.concatenate([center[24:], edge[24:]], axis=0),
        )

    def window(dyi, c, dx):
        return shifted[dyi, c, 8 + dx : 24 + dx, :]

    def applied(total, g, dyi, dx):
        out = []
        for f in range(F):
            gr_, gi_ = g[2 * f], g[2 * f + 1]
            ur, ui = window(dyi, 2 * f, dx), window(dyi, 2 * f + 1, dx)
            out.append(total[2 * f] + (gr_ * ur - gi_ * ui))
            out.append(total[2 * f + 1] + (gr_ * ui + gi_ * ur))
        return tuple(out)

    for copy in halo1:
        copy.wait_recv()
    shift_all(cbuf, lambda c: (edge_l[...], 8 * c, edge_r[...], 8 * c), 5)

    def couple(dyi, total):
        dy = dyi - H
        for dxi in range(SIDE):
            dx = dxi - H
            square = jnp.maximum(dx * dx + dy * dy, 1).astype(f32)
            rise = window(dyi, 4, dx) - hh
            dist2 = square + rise * rise
            inv = lax.rsqrt(dist2)
            inv = inv * (1.5 - 0.5 * dist2 * (inv * inv))
            bits = words[dxi // 4] >> (7 * (dxi % 4) + dyi)
            mag = jnp.where((bits & 1) == 1, 0.25 * inv, 0.0)
            s1, c1 = sincos((math.pi / 8) * (dist2 * inv) - 0.5 * math.pi)
            s1, c1 = c1, -s1
            c4, s4 = squared(*squared(c1, s1))
            g = (
                mag * c4,
                mag * s4,
                mag * (c4 * c1 - s4 * s1),
                mag * (s4 * c1 + c4 * s1),
            )
            for c in range(4):
                table[dyi, dxi, c] = g[c]
            total = applied(total, g, dyi, dx)
        return total

    def recouple(dyi, total):
        for dxi in range(SIDE):
            g = [table[dyi, dxi, c] for c in range(4)]
            total = applied(total, g, dyi, dxi - H)
        return total

    nothing = (jnp.zeros(wide, f32),) * 4
    near_old = lax.fori_loop(0, SIDE, couple, nothing)

    def times_z(f, real, imag):
        zr, zi = zin[2 * f], zin[2 * f + 1]
        return zr * real - zi * imag, zr * imag + zi * real

    def project(way, field, buf, send, recv):
        lj_even = (lane8 // 8) % 2 == 0
        for f in range(F):
            k = way * 4 + f * 2
            br, bi = base[k], base[k + 1]
            sr, si = field[2 * f], field[2 * f + 1]
            srcp[2 * f] = br * sr + bi * si
            srcp[2 * f + 1] = br * si - bi * sr

        def lay(r, carry):
            at = pl.ds(pl.multiple_of(r * XD, XD), XD)
            vc, vs = tab_v[0, :, at], tab_v[1, :, at]
            for f in range(F):
                sr = jnp.broadcast_to(srcp[2 * f, pl.ds(r, 1), :], small)
                si = jnp.broadcast_to(srcp[2 * f + 1, pl.ds(r, 1), :], small)
                both = jnp.concatenate([sr * vc - si * vs, sr * vs + si * vc], axis=0)
                high, low = split(both)
                tab_f_h[16 * f : 16 * f + 16, at] = high
                tab_f_l[16 * f : 16 * f + 16, at] = low
            return carry

        lax.fori_loop(0, RD, lay, 0)
        rows = slice(32 * way, 32 * way + 32)
        y = contract3(tab_u_h[rows, :], tab_u_l[rows, :], tab_f_h[...], tab_f_l[...])
        pad = jnp.zeros((8, 96), f32)
        yc = jnp.concatenate([y[0:8], pad], axis=1)
        ys = jnp.concatenate([y[16:24], pad], axis=1)
        sums = yc + jnp.where(lj_even, -pltpu.roll(ys, 120, 1), pltpu.roll(ys, 8, 1))
        for k in range(4):
            row = pick(sums, 8 * k + 7 - (lj & 7))
            row = jnp.where(sub8 == 7 - li, row, 0.0)
            buf[x, k : k + 1, :] = jnp.sum(row, axis=0, keepdims=True)
        spread_xr(buf, send, recv)

    for f in range(F):
        sr, si = times_z(f, inc[2 * f] - near_old[2 * f], inc[2 * f + 1] - near_old[2 * f + 1])
        loaded[2 * f] = sr
        loaded[2 * f + 1] = si
    project(0, loaded, fx, fxs, fxr)
    for c in range(4):
        cbuf2[c, 8:24, :] = loaded[c]
    pack_edges([loaded[c] for c in range(4)], pk_l2, pk_r2)
    halo2 = halo(cbuf2, edge_l2, edge_r2, pk_l2, pk_r2, hs2_sem, hr2_sem)
    for copy in halo2:
        copy.start()

    for g, height in enumerate(grouped(cbuf[4], sides(edge_l, edge_r, 4))):
        hs, hc = sincos_small(0.03 * height)
        c8, s8 = squared(*squared(*squared(hc, hs)))
        pwave[4, g] = c8 * wide_cell[4, g] - s8 * wide_cell[5, g]
        pwave[5, g] = s8 * wide_cell[4, g] + c8 * wide_cell[5, g]
        pwave[6, g] = hc * wide_cell[6, g] - hs * wide_cell[7, g]
        pwave[7, g] = hc * wide_cell[7, g] + hs * wide_cell[6, g]
        for f in range(F):
            k = 2 * f
            s, c = sincos((0.3 + 0.2 * f) * height)
            pwave[k, g] = c * wide_cell[k, g] - s * wide_cell[k + 1, g]
            pwave[k + 1, g] = s * wide_cell[k, g] + c * wide_cell[k + 1, g]
    for c in range(4):
        for g, value in enumerate(grouped(cbuf[5 + c], sides(edge_l, edge_r, 5 + c))):
            pz[c, g] = value

    await_bytes(gx.at[pl.ds(0, nx - 1)], gxr)
    g_sum = total_xr(gx)
    h0, h1 = regroup(g_sum[:8]), regroup(g_sum[8:])
    gmsg[0] = jnp.where(sub8 < 4, h0, pltpu.roll(h1, 4, 0))
    gmsg[1] = jnp.where(sub8 < 4, pltpu.roll(h0, 4, 0), h1)

    for to in blocks:
        pltpu.make_async_remote_copy(
            src_ref=gmsg.at[(to < d).astype(i32)], dst_ref=gr.at[d + 1],
            send_sem=grs, recv_sem=grr.at[d],
            device_id=(to, x), device_id_type=MESH,
        ).start()

    gr[d + 1] = gmsg[0]

    def send_feed(way, buf, recv, msg):
        await_bytes(buf.at[pl.ds(0, nx - 1)], recv)
        msg[...] = total_xr(buf)
        if way == 0:
            fr[d + 1] = msg[...]
        for to in blocks:

            @pl.when(to < d if way else to > d)
            def _():
                pltpu.make_async_remote_copy(
                    src_ref=msg, dst_ref=fr.at[d + 1], send_sem=frs, recv_sem=frr.at[d],
                    device_id=(to, x), device_id_type=MESH,
                ).start()

    def await_slots(buf, sem, first, last):
        def step(k, carry):
            await_bytes(buf.at[k + 1], sem.at[k])
            return carry

        lax.fori_loop(first, last, step, 0)

    def build(slot, first):
        if first:
            start = (7 - li) * 16 + sub8 - lj + 7
        else:
            start = (li + 7) * 16 + lj - sub8 + 7
        g = [
            [jnp.broadcast_to(gr[slot, r : r + 1, :], small) for r in (k, 4 + k)]
            for k in range(4)
        ]
        if not first:
            index = (lane8 & 7) * 16 + sub8
            shares = [pick(jnp.broadcast_to(tr[slot, f : f + 1, :], small), index) for f in range(F)]
            shares = jnp.where(lane8 < 8, shares[0], shares[1])
        for i in range(8):
            src = start + 16 * i if first else start - 16 * i
            index = src & 127
            near = src < 128
            m = [jnp.where(near, pick(g[k][0], index), pick(g[k][1], index)) for k in range(4)]
            own = lane8 == sub8 + 16 * i
            if not first:
                own = own | (lane8 == sub8 + (16 * i + 8))
            for f in range(F):
                mr, mi = m[2 * f], m[2 * f + 1]
                if first:
                    wr, wi = w_sub[2 * f, i], w_sub[2 * f + 1, i]
                else:
                    wr, wi = w_lane[2 * f], w_lane[2 * f + 1]
                real = jnp.where(own, 1.0, 0.0) - (mr * wr - mi * wi)
                imag = -(mr * wi + mi * wr)
                if not first:
                    at = 8 * f + i
                    share = jnp.broadcast_to(shares[:, at : at + 1], small)
                    real, imag = share * real, share * imag
                mats[slot, f, 0, i] = real
                mats[slot, f, 1, i] = imag

    def slots_of(way, t):
        if way == 0:
            at = 2 * t - lax.rem(d, 2)
            return at + 1, at + 2
        at = 2 * t - lax.rem(nd - 1 - d, 2)
        return nd - at, nd - at - 1

    def pairs_of(way):
        return (d + 1) // 2 if way == 0 else (nd - d) // 2

    def await_blocks(way, buf, sem):
        if way == 0:
            await_slots(buf, sem, 0, d)
        else:
            await_slots(buf, sem, d + 1, nd)

    def build_all(way):
        def step(t, carry):
            one, two = slots_of(way, t)
            build(one, True)
            build(two, False)
            return carry

        lax.fori_loop(0, pairs_of(way), step, 0)

    def tree(terms):
        while len(terms) > 1:
            terms = [a + b for a, b in zip(terms[::2], terms[1::2])]
        return terms[0]

    def carry_rows(one, f):
        real, imag = [], []
        for i in range(8):
            mr, mi = mats[one, f, 0, i], mats[one, f, 1, i]
            sr, si = state[1, f, 0, i], state[1, f, 1, i]
            real.append(mr * sr - mi * si)
            imag.append(mr * si + mi * sr)
        share = tr[one, f : f + 1, :]
        return [
            share * (jnp.sum(tree(terms), axis=0, keepdims=True) + fr[one, 2 * f + c : 2 * f + c + 1, :])
            for c, terms in enumerate((real, imag))
        ]

    def sweep(way):
        for f in range(F):
            for c in range(2):
                for i in range(8):
                    state[1, f, c, i] = zero8

        def step(t, carry):
            one, two = slots_of(way, t)
            for f in range(F):
                y = []
                for c, row in enumerate(carry_rows(one, f)):
                    k = 2 * f + c
                    near_rows[k : k + 1, :] = row
                    row = row + jnp.where(lj[:1] < 8, 0.0, fr[two, k : k + 1, :])
                    y.append(jnp.broadcast_to(row, small))
                yr, yi = y
                for i in range(8):
                    mr, mi = mats[two, f, 0, i], mats[two, f, 1, i]
                    vr = jnp.sum(mr * yr - mi * yi, axis=1, keepdims=True)
                    vi = jnp.sum(mr * yi + mi * yr, axis=1, keepdims=True)
                    state[1, f, 0, i] = jnp.broadcast_to(vr, small)
                    state[1, f, 1, i] = jnp.broadcast_to(vi, small)
            return carry

        lax.fori_loop(0, pairs_of(way), step, 0)

    def neighbour_carries():
        before = [jnp.broadcast_to(near_rows[k : k + 1, :], small) for k in range(4)]
        after = []
        for f in range(F):
            after += [jnp.broadcast_to(row, small) for row in carry_rows(d + 1, f)]
        for i in range(8):
            index = sub8 + 16 * i
            for f in range(F):
                for c in range(2):
                    state[0, f, c, i] = pick(before[2 * f + c], index)
                    state[2, f, c, i] = pick(after[2 * f + c], index)

    def weigh(which):
        for f in range(F):
            for i in range(8):
                wr, wi = w_sub[2 * f, i], w_sub[2 * f + 1, i]
                sr, si = state[which, f, 0, i], state[which, f, 1, i]
                state[which, f, 0, i] = wr * sr - wi * si
                state[which, f, 1, i] = wr * si + wi * sr

    def radiate(which, v, u, bases):
        vr, vi = v
        ur, ui = u

        def step(n, total):
            i = 7 - n
            out = []
            for f in range(F):
                tr, ti = total[2 * f], total[2 * f + 1]

                def coef(c, j):
                    return jnp.broadcast_to(state[which, f, c, i, j : j + 1, :], wide)

                ar, ai = coef(0, 7), coef(1, 7)
                for j in range(6, -1, -1):
                    ar, ai = ar * vr - ai * vi + coef(0, j), ar * vi + ai * vr + coef(1, j)
                out += [tr * ur - ti * ui + ar, tr * ui + ti * ur + ai]
            return tuple(out)

        total = lax.fori_loop(0, 8, step, nothing)
        out = []
        for f in range(F):
            br, bi = bases[2 * f], bases[2 * f + 1]
            tr, ti = total[2 * f], total[2 * f + 1]
            out += [br * tr - bi * ti, br * ti + bi * tr]
        return out

    send_feed(0, fx, fxr, fmsg)
    await_bytes(tr.at[pl.ds(0, nd - 1)], trr)
    await_blocks(0, gr, grr)
    build_all(0)
    build(d + 1, True)
    await_blocks(1, gr, grr)
    build_all(1)
    near_rows[...] = jnp.zeros((4, 128), f32)
    for copy in halo2:
        copy.wait_recv()
    for c in range(4):
        for g, value in enumerate(grouped(cbuf2[c], sides(edge_l2, edge_r2, c))):
            psrc[c, g] = value
    await_blocks(0, fr, frr)
    sweep(0)
    neighbour_carries()
    for which in range(3):
        weigh(which)
    for g in range(4):
        weak = radiate(
            (g + 1) // 2, (pwave[6, g], pwave[7, g]), (pwave[4, g], pwave[5, g]), [pwave[k, g] for k in range(4)]
        )
        for f in range(F):
            zr, zi = pz[2 * f, g], pz[2 * f + 1, g]
            wr, wi = weak[2 * f], weak[2 * f + 1]
            for c, flow in (
                (2 * f, psrc[2 * f, g] - (zr * wr - zi * wi)),
                (2 * f + 1, psrc[2 * f + 1, g] - (zr * wi + zi * wr)),
            ):
                if g == 1:
                    out_f[c] = flow
                    weakf[c] = weak[c]
                    cflow[c, 8:24, :] = flow
                elif g == 2:
                    eflow[c, 8:24, :] = flow
                else:
                    at = slice(0, 8) if g == 0 else slice(24, 32)
                    cflow[c, at, :] = flow[:8]
                    eflow[c, at, :] = flow[8:]
    shift_all(cflow, lambda c: (eflow[c], 0, eflow[c], 8), 4)
    near_new = lax.fori_loop(0, SIDE, recouple, nothing)
    for f in range(F):
        dr, di = times_z(
            f,
            inc[2 * f] - near_new[2 * f] - weakf[2 * f],
            inc[2 * f + 1] - near_new[2 * f + 1] - weakf[2 * f + 1],
        )
        driven[2 * f] = dr
        driven[2 * f + 1] = di
    project(1, driven, fx2, fxs2, fxr2)
    send_feed(1, fx2, fxr2, fmsg2)
    await_blocks(1, fr, frr)
    sweep(1)
    weigh(1)
    weak = radiate(1, (vu[0], vu[1]), (vu[4], vu[5]), [base[4 + k] for k in range(4)])
    for f in range(F):
        ar, ai = times_z(f, weak[2 * f], weak[2 * f + 1])
        out_c[2 * f] = driven[2 * f] - ar
        out_c[2 * f + 1] = driven[2 * f + 1] - ai

    for copy in halo1 + halo2:
        copy.wait_send()
    await_bytes(gx.at[pl.ds(0, nx - 1)], gxs)
    await_bytes(fx.at[pl.ds(0, nx - 1)], fxs)
    await_bytes(fx2.at[pl.ds(0, nx - 1)], fxs2)
    await_bytes(gr.at[pl.ds(0, nd - 1)], grs)
    await_bytes(fr.at[pl.ds(0, nd - 1)], frs)
    await_bytes(tr.at[pl.ds(0, nd - 1)], trs)


def solution(mesh):
    nd, nx = mesh.shape["rng"], mesh.shape["xr"]
    v_rows, u_rows, cell, wide = phase_tables()

    def per_device(incident, inverse_diag, previous, heights, neighbours, counts, transmit, angle_weights):
        vmem = pl.BlockSpec(memory_space=pltpu.VMEM)
        far = pl.BlockSpec(memory_space=pltpu.HBM)
        points = RD * XD
        V = pltpu.VMEM
        dma = pltpu.SemaphoreType.DMA
        held = [V(a.shape, a.dtype) for a in (
            incident, inverse_diag, previous, heights, neighbours, counts, transmit, angle_weights, v_rows
        )]
        scratch = held + [
            V((RD, 2, 16, XD), f32), V((12, RD, XD), f32),
            V((8, 4, RD, XD), f32), V((4, 4, RD, XD), f32), V((4, 4, RD, XD), f32), V((8, 4, RD, XD), f32),
            V((4, 32, XD), f32), V((4, 32, XD), f32), V((4, 128), f32),
            V((9, 32, XD), f32), V((32, XD), f32), V((32, XD), f32), V((RD, XD), f32), V((RD, XD), f32),
            V((4, 32, XD), f32), V((32, XD), f32), V((32, XD), f32), V((RD, XD), f32), V((RD, XD), f32),
            V((SIDE, 5, 32, XD), f32), V((SIDE, SIDE, 4, RD, XD), f32),
            V((64, points), bf16), V((64, points), bf16), V((64, points), bf16), V((64, points), bf16),
            V((2, 8, points), f32), V((32, points), bf16), V((32, points), bf16),
            V((4, RD, XD), f32), V((4, RD, XD), f32), V((4, RD, XD), f32), V((4, RD, XD), f32),
            V((4, 8, 128), f32), V((4, 8, 8, 128), f32), V((8, 128), f32), V((2, 128), f32), V((nd + 2, 2, 128), f32),
            V((nx, 16, 128), f32), V((2, 8, 128), f32), V((nd + 2, 8, 128), f32),
            V((nx, 4, 128), f32), V((nx, 4, 128), f32), V((4, 128), f32), V((4, 128), f32),
            V((nd + 2, 4, 128), f32), V((nd + 2, F, 2, 8, 8, 128), f32), V((3, F, 2, 8, 8, 128), f32),
            V((8, RD, XD), f32), V((6, RD, XD), f32),
            dma((12,)), dma((8,)), dma((8,)), dma((8,)), dma((8,)),
            dma, dma, dma, dma((nd,)), dma, dma, dma, dma, dma, dma((nd,)), dma, dma,
        ]
        return pl.pallas_call(
            functools.partial(kernel, nd, nx),
            out_shape=(V((2 * F, RD, XD), f32), V((2 * F, RD, XD), f32)),
            in_specs=[far] * 12,
            out_specs=(vmem, vmem),
            scratch_shapes=scratch,
            compiler_params=pltpu.CompilerParams(
                collective_id=0, has_side_effects=True, vmem_limit_bytes=60 << 20
            ),
        )(
            incident, inverse_diag, previous, heights, neighbours, counts, transmit, angle_weights,
            jnp.asarray(v_rows), jnp.asarray(u_rows), jnp.asarray(cell), jnp.asarray(wide),
        )

    placed = (
        P(None, "rng", "xr"),
        P(None, "rng", "xr"),
        P(None, "rng", "xr"),
        P("rng", "xr"),
        P(None, "rng", "xr"),
        P("rng", "xr"),
        P("rng", None, None),
        P(),
    )
    return jax.shard_map(
        per_device,
        mesh=mesh,
        in_specs=placed,
        out_specs=(P(None, "rng", "xr"), P(None, "rng", "xr")),
        check_vma=False,
    )
```

```python
import functools
import math

import jax
import jax.numpy as jnp
import numpy as np
from jax import lax
from jax.experimental import pallas as pl
from jax.experimental.pallas import tpu as pltpu
from jax.sharding import PartitionSpec as P

F = 2
Q = 64
H = 3
LMAX = 24
RD = 16
XD = 128
SIDE = 2 * H + 1
MESH = pl.DeviceIdType.MESH
f32 = jnp.float32
bf16 = jnp.bfloat16
i32 = jnp.int32


def phase_tables():
    turn = 2.0 * math.pi / 64
    power = np.arange(16) - 7
    cols = np.arange(XD)
    ang = turn * ((power[:, None] * cols[None, :]) % 64)
    v_rows = np.stack([np.cos(ang), np.sin(ang)]).astype(np.float32)
    u_rows = np.zeros((4, RD, 2, 16, XD), np.float32)
    cell = np.zeros((4, 12, RD, XD), np.float32)
    for dm in range(4):
        rows = 16 * dm + np.arange(RD)
        ang = turn * ((power[None, :] * rows[:, None]) % 64)
        u_rows[dm, :, 0] = np.cos(ang)[:, :, None]
        u_rows[dm, :, 1] = np.sin(ang)[:, :, None]
        for way, sign in enumerate((1, -1)):
            for f in range(F):
                ang = turn * ((sign * (1 + 2 * f) * rows[:, None] + (f - 4) * cols[None, :]) % 64)
                cell[dm, way * 4 + f * 2] = np.cos(ang)
                cell[dm, way * 4 + f * 2 + 1] = np.sin(ang)
        ang = turn * ((rows[:, None] + 0 * cols[None, :]) % 64)
        cell[dm, 8], cell[dm, 9] = np.cos(ang), np.sin(ang)
        ang = turn * ((0 * rows[:, None] + cols[None, :]) % 64)
        cell[dm, 10], cell[dm, 11] = np.cos(ang), np.sin(ang)
    lane = np.arange(XD)
    side = np.where(lane < 8, lane - 3, lane + 120)
    wide = np.zeros((4, 8, 4, RD, XD), np.float32)
    for dm in range(4):
        rows = 16 * dm - 8 + np.arange(32)
        row_at = np.stack([np.r_[rows[:8], rows[:8]], rows[8:24], rows[8:24], np.r_[rows[24:], rows[24:]]])
        half = np.concatenate([np.tile(lane, (8, 1)), np.tile(side, (8, 1))])
        col_at = np.stack([half, np.tile(lane, (RD, 1)), np.tile(side, (RD, 1)), half])
        row_at = row_at[:, :, None] + 0 * col_at
        angs = [(1 + 2 * f) * row_at + (f - 4) * col_at for f in range(F)] + [row_at, col_at]
        for n, ang in enumerate(angs):
            wide[dm, 2 * n] = np.cos(turn * (ang % 64))
            wide[dm, 2 * n + 1] = np.sin(turn * (ang % 64))
    return v_rows, u_rows, cell, wide


def sincos_small(t):
    q = t * t
    s = t * (1.0 + q * (-1.0 / 6 + q * (1.0 / 120 + q * (-1.0 / 5040 + q * (1.0 / 362880)))))
    c = 1.0 + q * (-0.5 + q * (1.0 / 24 + q * (-1.0 / 720 + q * (1.0 / 40320))))
    return s, c


def sincos(t):
    q = t * t
    s = t * (
        1.0
        + q
        * (
            -1.0 / 6
            + q * (1.0 / 120 + q * (-1.0 / 5040 + q * (1.0 / 362880 + q * (-1.0 / 39916800))))
        )
    )
    c = 1.0 + q * (
        -0.5
        + q
        * (
            1.0 / 24
            + q
            * (-1.0 / 720 + q * (1.0 / 40320 + q * (-1.0 / 3628800 + q * (1.0 / 479001600))))
        )
    )
    return s, c


def squared(c, s):
    return c * c - s * s, 2.0 * (c * s)


def lanes_of(shape):
    return lax.broadcasted_iota(i32, shape, 1)


def rows_of(shape):
    return lax.broadcasted_iota(i32, shape, 0)


def pick(value, index):
    return jnp.take_along_axis(value, index, axis=1, mode="promise_in_bounds")


def split(value):
    high = value.astype(bf16)
    return high, (value - high.astype(f32)).astype(bf16)


def contract(left, right):
    return lax.dot_general(left, right, (((1,), (1,)), ((), ())), preferred_element_type=f32)


def contract3(left_high, left_low, right_high, right_low):
    return (
        contract(left_high, right_high)
        + contract(left_high, right_low)
        + contract(left_low, right_high)
    )


def regroup(value):
    shape = (8, 128)
    part = (rows_of(shape) - lanes_of(shape) // 16) & 7
    out = jnp.zeros(shape, f32)
    for s in range(8):
        moved = value
        if s:
            moved = pltpu.roll(pltpu.roll(value, 128 - 16 * s, 1), s, 0)
        out = jnp.where(part == s, moved, out)
    return out


def kernel(
    nd, nx,
    inc_hbm, zin_hbm, prev_hbm, hts_hbm, nbr_hbm, cnt_hbm, trn_hbm, aw_hbm, v_hbm, u_hbm, cell_hbm, wide_hbm,
    out_f, out_c,
    inc, zin, prev, hts, nbr, cnt, trn, aw, v_rows, u_rows, cell, wide_cell, pz, psrc, pwave, cflow, eflow, near_rows, cbuf, edge_l, edge_r, pk_l, pk_r,
    cbuf2, edge_l2, edge_r2, pk_l2, pk_r2,
    shifted, table, tab_u_h, tab_u_l, tab_a_h, tab_a_l, tab_v, tab_f_h, tab_f_l,
    srcp, loaded, driven, weakf, w_lane, w_sub, row_buf, share_msg, tr, tb,
    gx, gmsg, gr, fx, fx2, fmsg, fmsg2, fr, mats, state,
    base, vu,
    csem, hs_sem, hr_sem, hs2_sem, hr2_sem,
    gxs, gxr, grs, grr, fxs, fxr, fxs2, fxr2, frs, frr, trs, trr,
):
    d = lax.axis_index("rng")
    x = lax.axis_index("xr")
    dm = lax.rem(d, 4)
    spread = 1.0 / math.sqrt(RD * XD * nx)
    up, down = lax.rem(d + nd - 1, nd), lax.rem(d + 1, nd)
    left, right = lax.rem(x + nx - 1, nx), lax.rem(x + 1, nx)

    def turned(value, by, size):
        moved = value + by
        return jnp.where(moved >= size, moved - size, moved)

    nc = min(4, nd)
    nr = nd // nc
    far = lambda n, size: min(n, size - n)
    others = sorted(
        ((a, b) for a in range(nr) for b in range(nc) if a or b),
        key=lambda p: -far(p[0], nr) - far(p[1], nc),
    )
    d_row, d_col = d // nc, lax.rem(d, nc)
    blocks = [turned(d_row, a, nr) * nc + turned(d_col, b, nc) for a, b in others]
    owners = [turned(x, n, nx) for n in sorted(range(1, nx), key=lambda n: -far(n, nx))]

    barrier = pltpu.get_barrier_semaphore()
    peers = [(to, x) for to in blocks] + [(d, to) for to in owners]
    peers += [(dd, xx) for dd in (up, down) for xx in (left, right)]
    for peer in peers:
        pl.semaphore_signal(barrier, inc=1, device_id=peer, device_id_type=MESH)

    fetches = [
        (prev_hbm, prev), (hts_hbm, hts), (zin_hbm, zin), (trn_hbm, trn), (v_hbm, v_rows), (u_hbm.at[dm], u_rows),
        (aw_hbm, aw), (cell_hbm.at[dm], cell), (cnt_hbm, cnt), (nbr_hbm, nbr), (inc_hbm, inc),
        (wide_hbm.at[dm], wide_cell),
    ]
    fetches = [pltpu.make_async_copy(a, b, csem.at[n]) for n, (a, b) in enumerate(fetches)]
    for fetch in fetches:
        fetch.start()

    wide = (RD, XD)
    lane16 = lanes_of(wide)
    small = (8, 128)
    lane8 = lanes_of(small)
    sub8 = rows_of(small)

    def pack_edges(parts, to_left, to_right):
        a = jnp.zeros(wide, f32)
        b = jnp.zeros(wide, f32)
        for c, part in enumerate(parts):
            here = lane16 // 8 == c
            a = jnp.where(here, part if c == 0 else pltpu.roll(part, 8 * c, 1), a)
            b = jnp.where(here, pltpu.roll(part, 8 * c + 3, 1), b)
        to_left[...] = a
        to_right[...] = b

    for fetch in fetches[:3]:
        fetch.wait()
    for c in range(4):
        cbuf[c, 8:24, :] = prev[c]
        cbuf[5 + c, 8:24, :] = zin[c]
    cbuf[4, 8:24, :] = hts[...]
    pack_edges([prev[c] for c in range(4)] + [hts[...]] + [zin[c] for c in range(4)], pk_l, pk_r)
    zero8 = jnp.zeros(small, f32)
    li, lj = lane8 // 16, lane8 % 16
    for slot in (0, nd + 1):
        gr[slot] = zero8
        fr[slot] = jnp.zeros((4, 128), f32)
        tr[slot] = jnp.zeros((2, 128), f32)
    fetches[3].wait()
    row_buf[...] = zero8
    row_buf[4:6, 0:Q] = trn[0]
    share_rows = jnp.where(lj < 8, pick(row_buf[...], (li * 8 + lj) & 127), 0.0)
    share_msg[...] = share_rows[4:6, :]
    tr[d + 1] = share_rows[4:6, :]

    def halo(buf, e_l, e_r, p_l, p_r, send, recv):
        plan = [
            (p_l.at[0:8, :], e_r.at[24:32, :], (up, left)),
            (p_l.at[8:16, :], e_r.at[0:8, :], (down, left)),
            (p_r.at[0:8, :], e_l.at[24:32, :], (up, right)),
            (p_r.at[8:16, :], e_l.at[0:8, :], (down, right)),
            (buf.at[:, 8:16, :], buf.at[:, 24:32, :], (up, x)),
            (buf.at[:, 16:24, :], buf.at[:, 0:8, :], (down, x)),
            (p_l, e_r.at[8:24, :], (d, left)),
            (p_r, e_l.at[8:24, :], (d, right)),
        ]
        return [
            pltpu.make_async_remote_copy(
                src_ref=src, dst_ref=dst, send_sem=send.at[n], recv_sem=recv.at[n],
                device_id=dev, device_id_type=MESH,
            )
            for n, (src, dst, dev) in enumerate(plan)
        ]

    for fetch in fetches[4:6]:
        fetch.wait()
    power16 = (rows_of(wide) - 7).astype(f32) * 0.03

    def fill(r, carry):
        at = pl.ds(pl.multiple_of(r * XD, XD), XD)
        hrow = jnp.broadcast_to(hts[pl.ds(r, 1), :], wide)
        hs, hc = sincos_small(power16 * hrow)
        vc0, vs0 = v_rows[0], v_rows[1]
        vc = hc * vc0 - hs * vs0
        vs = hc * vs0 + hs * vc0
        tab_v[0, :, at] = vc[:8]
        tab_v[1, :, at] = vs[:8]
        c8, s8 = squared(*squared(*squared(hc, hs)))
        pc, ps = u_rows[r, 0], u_rows[r, 1]
        cc_, ss_, cs_, sc_ = c8 * pc, s8 * ps, c8 * ps, s8 * pc
        for n, value in enumerate((cc_ - ss_, sc_ + cs_, cc_ + ss_, sc_ - cs_)):
            high, low = split(value)
            tab_u_h[16 * n : 16 * n + 16, at] = high
            tab_u_l[16 * n : 16 * n + 16, at] = low
        for f in range(F):
            zr = jnp.broadcast_to(zin[2 * f, pl.ds(r, 1), :], wide)
            zi = jnp.broadcast_to(zin[2 * f + 1, pl.ds(r, 1), :], wide)
            for n, value in enumerate((zr * vc - zi * vs, zr * vs + zi * vc)):
                high, low = split(value)
                k = 2 * f + n
                tab_a_h[16 * k : 16 * k + 16, at] = high
                tab_a_l[16 * k : 16 * k + 16, at] = low
        return carry

    lax.fori_loop(0, RD, fill, 0)

    y = contract3(tab_u_h[...], tab_u_l[...], tab_a_h[...], tab_a_l[...])
    yc = jnp.concatenate([y[0:16], y[32:48]], axis=1)
    ys = jnp.concatenate([y[16:32], y[48:64]], axis=1)
    gx[x] = yc + jnp.where((lane16 // 16) % 2 == 0, -pltpu.roll(ys, 112, 1), pltpu.roll(ys, 16, 1))

    def spread_xr(buf, send, recv):
        for to in owners:
            pltpu.make_async_remote_copy(
                src_ref=buf.at[x], dst_ref=buf.at[x], send_sem=send, recv_sem=recv,
                device_id=(d, to), device_id_type=MESH,
            ).start()

    def await_bytes(view, sem):
        pltpu.make_async_copy(view, view, sem).wait()

    def total_xr(buf):
        total = buf[0]
        for k in range(1, nx):
            total = total + buf[k]
        return total

    pl.semaphore_wait(barrier, nd - 1 + nx - 1 + 4)
    halo1 = halo(cbuf, edge_l, edge_r, pk_l, pk_r, hs_sem, hr_sem)
    for copy in halo1:
        copy.start()
    for to in blocks:
        pltpu.make_async_remote_copy(
            src_ref=share_msg, dst_ref=tr.at[d + 1], send_sem=trs, recv_sem=trr,
            device_id=(to, x), device_id_type=MESH,
        ).start()
    spread_xr(gx, gxs, gxr)

    for fetch in fetches[6:]:
        fetch.wait()
    for f in range(F):
        for c in range(2):
            row_buf[2 * f + c : 2 * f + c + 1, 0:Q] = aw[f, c : c + 1, :]
    weight_rows = [jnp.broadcast_to(row_buf[k : k + 1, :], small) * spread for k in range(4)]
    for k in range(4):
        w_lane[k] = jnp.where(lj < 8, pick(weight_rows[k], (li * 8 + lj) & 127), 0.0)
    for i in range(8):
        for k in range(4):
            w_sub[k, i] = pick(weight_rows[k], sub8 + 8 * i)

    hh = hts[...]
    hs, hc = sincos_small(0.03 * hh)
    c8, s8 = squared(*squared(*squared(hc, hs)))
    vu[0] = hc * cell[10] - hs * cell[11]
    vu[1] = hc * cell[11] + hs * cell[10]
    vu[2] = c8 * cell[8] - s8 * cell[9]
    vu[3] = s8 * cell[8] + c8 * cell[9]
    vu[4] = c8 * cell[8] + s8 * cell[9]
    vu[5] = s8 * cell[8] - c8 * cell[9]
    for f in range(F):
        s, c = sincos((0.3 + 0.2 * f) * hh)
        for way in range(2):
            k = way * 4 + f * 2
            base[k] = c * cell[k] - s * cell[k + 1]
            base[k + 1] = s * cell[k] + c * cell[k + 1]

    def note(l, words):
        word0, word1 = words
        code = nbr[l]
        m = jnp.where(code >= 24, code + 1, code)
        low = m < 28
        bit = jnp.where(l < cnt[...], jnp.left_shift(1, jnp.where(low, m, m - 28)), 0)
        return word0 | jnp.where(low, bit, 0), word1 | jnp.where(low, 0, bit)

    zero_word = jnp.zeros(wide, i32)
    words = lax.fori_loop(0, LMAX, note, (zero_word, zero_word))

    tall = (32, XD)
    lane32 = lanes_of(tall)
    row32 = rows_of(tall) + (d * RD - 8)
    inside = (row32 >= 0) & (row32 < nd * RD)

    def shift_all(buf, edges, count):
        to_left = inside & (lane32 < 128 * x)
        to_right = inside & (lane32 < 128 * (nx - 1 - x))
        for c in range(count):
            el, left_at, er, right_at = edges(c)
            el = jnp.where(to_left, el, 0.0)
            er = jnp.where(to_right, er, 0.0)
            mid = jnp.where(inside, buf[c], 0.0)
            shifted[H, c] = mid
            for k in range(1, H + 1):
                shifted[H + k, c] = jnp.where(
                    lane32 >= 128 - k,
                    pltpu.roll(er, (128 - k - right_at) % 128, 1),
                    pltpu.roll(mid, 128 - k, 1),
                )
                shifted[H - k, c] = jnp.where(
                    lane32 < k,
                    pltpu.roll(el, (k - 3 - left_at) % 128, 1),
                    pltpu.roll(mid, k, 1),
                )

    def sides(e_l, e_r, c):
        left_part = e_l[...] if c == 0 else pltpu.roll(e_l[...], 128 - 8 * c, 1)
        right_part = e_r[...] if c == 1 else pltpu.roll(e_r[...], (136 - 8 * c) % 128, 1)
        return jnp.where(lane32 < 8, left_part, right_part)

    def grouped(center, edge):
        return (
            jnp.concatenate([center[:8], edge[:8]], axis=0),
            center[8:24],
            edge[8:24],
            jnp.concatenate([center[24:], edge[24:]], axis=0),
        )

    def window(dyi, c, dx):
        return shifted[dyi, c, 8 + dx : 24 + dx, :]

    def applied(total, g, dyi, dx):
        out = []
        for f in range(F):
            gr_, gi_ = g[2 * f], g[2 * f + 1]
            ur, ui = window(dyi, 2 * f, dx), window(dyi, 2 * f + 1, dx)
            out.append(total[2 * f] + (gr_ * ur - gi_ * ui))
            out.append(total[2 * f + 1] + (gr_ * ui + gi_ * ur))
        return tuple(out)

    for copy in halo1:
        copy.wait_recv()
    shift_all(cbuf, lambda c: (edge_l[...], 8 * c, edge_r[...], 8 * c), 5)

    def couple(dyi, total):
        dy = dyi - H
        for dxi in range(SIDE):
            dx = dxi - H
            square = jnp.maximum(dx * dx + dy * dy, 1).astype(f32)
            rise = window(dyi, 4, dx) - hh
            dist2 = square + rise * rise
            inv = lax.rsqrt(dist2)
            inv = inv * (1.5 - 0.5 * dist2 * (inv * inv))
            bits = words[dxi // 4] >> (7 * (dxi % 4) + dyi)
            mag = jnp.where((bits & 1) == 1, 0.25 * inv, 0.0)
            s1, c1 = sincos((math.pi / 8) * (dist2 * inv) - 0.5 * math.pi)
            s1, c1 = c1, -s1
            c4, s4 = squared(*squared(c1, s1))
            g = (
                mag * c4,
                mag * s4,
                mag * (c4 * c1 - s4 * s1),
                mag * (s4 * c1 + c4 * s1),
            )
            for c in range(4):
                table[dyi, dxi, c] = g[c]
            total = applied(total, g, dyi, dx)
        return total

    def recouple(dyi, total):
        for dxi in range(SIDE):
            g = [table[dyi, dxi, c] for c in range(4)]
            total = applied(total, g, dyi, dxi - H)
        return total

    nothing = (jnp.zeros(wide, f32),) * 4
    near_old = lax.fori_loop(0, SIDE, couple, nothing)

    def times_z(f, real, imag):
        zr, zi = zin[2 * f], zin[2 * f + 1]
        return zr * real - zi * imag, zr * imag + zi * real

    def project(way, field, buf, send, recv):
        lj_even = (lane8 // 8) % 2 == 0
        for f in range(F):
            k = way * 4 + f * 2
            br, bi = base[k], base[k + 1]
            sr, si = field[2 * f], field[2 * f + 1]
            srcp[2 * f] = br * sr + bi * si
            srcp[2 * f + 1] = br * si - bi * sr

        def lay(r, carry):
            at = pl.ds(pl.multiple_of(r * XD, XD), XD)
            vc, vs = tab_v[0, :, at], tab_v[1, :, at]
            for f in range(F):
                sr = jnp.broadcast_to(srcp[2 * f, pl.ds(r, 1), :], small)
                si = jnp.broadcast_to(srcp[2 * f + 1, pl.ds(r, 1), :], small)
                both = jnp.concatenate([sr * vc - si * vs, sr * vs + si * vc], axis=0)
                high, low = split(both)
                tab_f_h[16 * f : 16 * f + 16, at] = high
                tab_f_l[16 * f : 16 * f + 16, at] = low
            return carry

        lax.fori_loop(0, RD, lay, 0)
        rows = slice(32 * way, 32 * way + 32)
        y = contract3(tab_u_h[rows, :], tab_u_l[rows, :], tab_f_h[...], tab_f_l[...])
        pad = jnp.zeros((8, 96), f32)
        yc = jnp.concatenate([y[0:8], pad], axis=1)
        ys = jnp.concatenate([y[16:24], pad], axis=1)
        sums = yc + jnp.where(lj_even, -pltpu.roll(ys, 120, 1), pltpu.roll(ys, 8, 1))
        for k in range(4):
            row = pick(sums, 8 * k + 7 - (lj & 7))
            row = jnp.where(sub8 == 7 - li, row, 0.0)
            buf[x, k : k + 1, :] = jnp.sum(row, axis=0, keepdims=True)
        spread_xr(buf, send, recv)

    for f in range(F):
        sr, si = times_z(f, inc[2 * f] - near_old[2 * f], inc[2 * f + 1] - near_old[2 * f + 1])
        loaded[2 * f] = sr
        loaded[2 * f + 1] = si
    project(0, loaded, fx, fxs, fxr)
    await_bytes(gx.at[pl.ds(0, nx - 1)], gxr)
    g_sum = total_xr(gx)
    h0, h1 = regroup(g_sum[:8]), regroup(g_sum[8:])
    gmsg[0] = jnp.where(sub8 < 4, h0, pltpu.roll(h1, 4, 0))
    gmsg[1] = jnp.where(sub8 < 4, pltpu.roll(h0, 4, 0), h1)

    for to in blocks:
        pltpu.make_async_remote_copy(
            src_ref=gmsg.at[(to < d).astype(i32)], dst_ref=gr.at[d + 1],
            send_sem=grs, recv_sem=grr.at[d],
            device_id=(to, x), device_id_type=MESH,
        ).start()

    gr[d + 1] = gmsg[0]

    for c in range(4):
        cbuf2[c, 8:24, :] = loaded[c]
    pack_edges([loaded[c] for c in range(4)], pk_l2, pk_r2)
    halo2 = halo(cbuf2, edge_l2, edge_r2, pk_l2, pk_r2, hs2_sem, hr2_sem)
    for copy in halo2:
        copy.start()

    for g, height in enumerate(grouped(cbuf[4], sides(edge_l, edge_r, 4))):
        hs, hc = sincos_small(0.03 * height)
        c8, s8 = squared(*squared(*squared(hc, hs)))
        pwave[4, g] = c8 * wide_cell[4, g] - s8 * wide_cell[5, g]
        pwave[5, g] = s8 * wide_cell[4, g] + c8 * wide_cell[5, g]
        pwave[6, g] = hc * wide_cell[6, g] - hs * wide_cell[7, g]
        pwave[7, g] = hc * wide_cell[7, g] + hs * wide_cell[6, g]
        for f in range(F):
            k = 2 * f
            s, c = sincos((0.3 + 0.2 * f) * height)
            pwave[k, g] = c * wide_cell[k, g] - s * wide_cell[k + 1, g]
            pwave[k + 1, g] = s * wide_cell[k, g] + c * wide_cell[k + 1, g]
    for c in range(4):
        for g, value in enumerate(grouped(cbuf[5 + c], sides(edge_l, edge_r, 5 + c))):
            pz[c, g] = value

    await_bytes(tr.at[pl.ds(0, nd - 1)], trr)

    def spread_shares(n, carry):
        for k in range(4):
            slot = 4 * n + (k + 1)
            index = (lane8 & 7) * 16 + sub8
            two = [pick(jnp.broadcast_to(tr[slot, f : f + 1, :], small), index) for f in range(F)]
            two = jnp.where(lane8 < 8, two[0], two[1])
            for at in range(16):
                tb[slot, at] = jnp.broadcast_to(two[:, at : at + 1], small)
        return carry

    lax.fori_loop(0, nd // 4, spread_shares, 0)

    def send_feed(way, buf, recv, msg):
        await_bytes(buf.at[pl.ds(0, nx - 1)], recv)
        msg[...] = total_xr(buf)
        if way == 0:
            fr[d + 1] = msg[...]
        for to in blocks:

            @pl.when(to < d if way else to > d)
            def _():
                pltpu.make_async_remote_copy(
                    src_ref=msg, dst_ref=fr.at[d + 1], send_sem=frs, recv_sem=frr.at[d],
                    device_id=(to, x), device_id_type=MESH,
                ).start()

    def await_slots(buf, sem, first, last):
        def step(k, carry):
            await_bytes(buf.at[k + 1], sem.at[k])
            return carry

        lax.fori_loop(first, last, step, 0)

    def build(slot, first):
        if first:
            start = (7 - li) * 16 + sub8 - lj + 7
        else:
            start = (li + 7) * 16 + lj - sub8 + 7
        g = [
            [jnp.broadcast_to(gr[slot, r : r + 1, :], small) for r in (k, 4 + k)]
            for k in range(4)
        ]
        for i in range(8):
            src = start + 16 * i if first else start - 16 * i
            index = src & 127
            near = src < 128
            m = [jnp.where(near, pick(g[k][0], index), pick(g[k][1], index)) for k in range(4)]
            own = lane8 == sub8 + 16 * i
            if not first:
                own = own | (lane8 == sub8 + (16 * i + 8))
            for f in range(F):
                mr, mi = m[2 * f], m[2 * f + 1]
                if first:
                    wr, wi = w_sub[2 * f, i], w_sub[2 * f + 1, i]
                else:
                    wr, wi = w_lane[2 * f], w_lane[2 * f + 1]
                real = jnp.where(own, 1.0, 0.0) - (mr * wr - mi * wi)
                imag = -(mr * wi + mi * wr)
                if not first:
                    share = tb[slot, 8 * f + i]
                    real, imag = share * real, share * imag
                mats[slot, f, 0, i] = real
                mats[slot, f, 1, i] = imag

    def slots_of(way, t):
        if way == 0:
            at = 2 * t - lax.rem(d, 2)
            return at + 1, at + 2
        at = 2 * t - lax.rem(nd - 1 - d, 2)
        return nd - at, nd - at - 1

    def pairs_of(way):
        return (d + 1) // 2 if way == 0 else (nd - d) // 2

    def await_blocks(way, buf, sem):
        if way == 0:
            await_slots(buf, sem, 0, d)
        else:
            await_slots(buf, sem, d + 1, nd)

    def build_all(way):
        def step(t, carry):
            one, two = slots_of(way, t)
            build(one, True)
            build(two, False)
            return carry

        lax.fori_loop(0, pairs_of(way), step, 0)

    def tree(terms):
        while len(terms) > 1:
            terms = [a + b for a, b in zip(terms[::2], terms[1::2])]
        return terms[0]

    def carry_rows(one, f):
        real, imag = [], []
        for i in range(8):
            mr, mi = mats[one, f, 0, i], mats[one, f, 1, i]
            sr, si = state[1, f, 0, i], state[1, f, 1, i]
            real.append(mr * sr - mi * si)
            imag.append(mr * si + mi * sr)
        share = tr[one, f : f + 1, :]
        return [
            share * (jnp.sum(tree(terms), axis=0, keepdims=True) + fr[one, 2 * f + c : 2 * f + c + 1, :])
            for c, terms in enumerate((real, imag))
        ]

    def sweep(way):
        for f in range(F):
            for c in range(2):
                for i in range(8):
                    state[1, f, c, i] = zero8

        def step(t, carry):
            one, two = slots_of(way, t)
            for f in range(F):
                y = []
                for c, row in enumerate(carry_rows(one, f)):
                    k = 2 * f + c
                    near_rows[k : k + 1, :] = row
                    row = row + jnp.where(lj[:1] < 8, 0.0, fr[two, k : k + 1, :])
                    y.append(jnp.broadcast_to(row, small))
                yr, yi = y
                for i in range(8):
                    mr, mi = mats[two, f, 0, i], mats[two, f, 1, i]
                    vr = jnp.sum(mr * yr - mi * yi, axis=1, keepdims=True)
                    vi = jnp.sum(mr * yi + mi * yr, axis=1, keepdims=True)
                    state[1, f, 0, i] = jnp.broadcast_to(vr, small)
                    state[1, f, 1, i] = jnp.broadcast_to(vi, small)
            return carry

        lax.fori_loop(0, pairs_of(way), step, 0)

    def neighbour_carries():
        before = [jnp.broadcast_to(near_rows[k : k + 1, :], small) for k in range(4)]
        after = []
        for f in range(F):
            after += [jnp.broadcast_to(row, small) for row in carry_rows(d + 1, f)]
        for i in range(8):
            index = sub8 + 16 * i
            for f in range(F):
                for c in range(2):
                    state[0, f, c, i] = pick(before[2 * f + c], index)
                    state[2, f, c, i] = pick(after[2 * f + c], index)

    def weigh(which):
        for f in range(F):
            for i in range(8):
                wr, wi = w_sub[2 * f, i], w_sub[2 * f + 1, i]
                sr, si = state[which, f, 0, i], state[which, f, 1, i]
                state[which, f, 0, i] = wr * sr - wi * si
                state[which, f, 1, i] = wr * si + wi * sr

    def radiate(which, v, u, bases):
        vr, vi = v
        ur, ui = u

        def step(n, total):
            i = 7 - n
            out = []
            for f in range(F):
                tr, ti = total[2 * f], total[2 * f + 1]

                def coef(c, j):
                    return jnp.broadcast_to(state[which, f, c, i, j : j + 1, :], wide)

                ar, ai = coef(0, 7), coef(1, 7)
                for j in range(6, -1, -1):
                    ar, ai = ar * vr - ai * vi + coef(0, j), ar * vi + ai * vr + coef(1, j)
                out += [tr * ur - ti * ui + ar, tr * ui + ti * ur + ai]
            return tuple(out)

        total = lax.fori_loop(0, 8, step, nothing)
        out = []
        for f in range(F):
            br, bi = bases[2 * f], bases[2 * f + 1]
            tr, ti = total[2 * f], total[2 * f + 1]
            out += [br * tr - bi * ti, br * ti + bi * tr]
        return out

    send_feed(0, fx, fxr, fmsg)
    await_blocks(0, gr, grr)
    build_all(0)
    build(d + 1, True)
    await_blocks(1, gr, grr)
    build_all(1)
    near_rows[...] = jnp.zeros((4, 128), f32)
    for copy in halo2:
        copy.wait_recv()
    for c in range(4):
        for g, value in enumerate(grouped(cbuf2[c], sides(edge_l2, edge_r2, c))):
            psrc[c, g] = value
    await_blocks(0, fr, frr)
    sweep(0)
    neighbour_carries()
    for which in range(3):
        weigh(which)
    for g in range(4):
        weak = radiate(
            (g + 1) // 2, (pwave[6, g], pwave[7, g]), (pwave[4, g], pwave[5, g]), [pwave[k, g] for k in range(4)]
        )
        for f in range(F):
            zr, zi = pz[2 * f, g], pz[2 * f + 1, g]
            wr, wi = weak[2 * f], weak[2 * f + 1]
            for c, flow in (
                (2 * f, psrc[2 * f, g] - (zr * wr - zi * wi)),
                (2 * f + 1, psrc[2 * f + 1, g] - (zr * wi + zi * wr)),
            ):
                if g == 1:
                    out_f[c] = flow
                    weakf[c] = weak[c]
                    cflow[c, 8:24, :] = flow
                elif g == 2:
                    eflow[c, 8:24, :] = flow
                else:
                    at = slice(0, 8) if g == 0 else slice(24, 32)
                    cflow[c, at, :] = flow[:8]
                    eflow[c, at, :] = flow[8:]
    shift_all(cflow, lambda c: (eflow[c], 0, eflow[c], 8), 4)
    near_new = lax.fori_loop(0, SIDE, recouple, nothing)
    for f in range(F):
        dr, di = times_z(
            f,
            inc[2 * f] - near_new[2 * f] - weakf[2 * f],
            inc[2 * f + 1] - near_new[2 * f + 1] - weakf[2 * f + 1],
        )
        driven[2 * f] = dr
        driven[2 * f + 1] = di
    project(1, driven, fx2, fxs2, fxr2)
    send_feed(1, fx2, fxr2, fmsg2)
    await_blocks(1, fr, frr)
    sweep(1)
    weigh(1)
    weak = radiate(1, (vu[0], vu[1]), (vu[4], vu[5]), [base[4 + k] for k in range(4)])
    for f in range(F):
        ar, ai = times_z(f, weak[2 * f], weak[2 * f + 1])
        out_c[2 * f] = driven[2 * f] - ar
        out_c[2 * f + 1] = driven[2 * f + 1] - ai

    for copy in halo1 + halo2:
        copy.wait_send()
    await_bytes(gx.at[pl.ds(0, nx - 1)], gxs)
    await_bytes(fx.at[pl.ds(0, nx - 1)], fxs)
    await_bytes(fx2.at[pl.ds(0, nx - 1)], fxs2)
    await_bytes(gr.at[pl.ds(0, nd - 1)], grs)
    await_bytes(fr.at[pl.ds(0, nd - 1)], frs)
    await_bytes(tr.at[pl.ds(0, nd - 1)], trs)


def solution(mesh):
    nd, nx = mesh.shape["rng"], mesh.shape["xr"]
    v_rows, u_rows, cell, wide = phase_tables()

    def per_device(incident, inverse_diag, previous, heights, neighbours, counts, transmit, angle_weights):
        vmem = pl.BlockSpec(memory_space=pltpu.VMEM)
        far = pl.BlockSpec(memory_space=pltpu.HBM)
        points = RD * XD
        V = pltpu.VMEM
        dma = pltpu.SemaphoreType.DMA
        held = [V(a.shape, a.dtype) for a in (
            incident, inverse_diag, previous, heights, neighbours, counts, transmit, angle_weights, v_rows
        )]
        scratch = held + [
            V((RD, 2, 16, XD), f32), V((12, RD, XD), f32),
            V((8, 4, RD, XD), f32), V((4, 4, RD, XD), f32), V((4, 4, RD, XD), f32), V((8, 4, RD, XD), f32),
            V((4, 32, XD), f32), V((4, 32, XD), f32), V((4, 128), f32),
            V((9, 32, XD), f32), V((32, XD), f32), V((32, XD), f32), V((RD, XD), f32), V((RD, XD), f32),
            V((4, 32, XD), f32), V((32, XD), f32), V((32, XD), f32), V((RD, XD), f32), V((RD, XD), f32),
            V((SIDE, 5, 32, XD), f32), V((SIDE, SIDE, 4, RD, XD), f32),
            V((64, points), bf16), V((64, points), bf16), V((64, points), bf16), V((64, points), bf16),
            V((2, 8, points), f32), V((32, points), bf16), V((32, points), bf16),
            V((4, RD, XD), f32), V((4, RD, XD), f32), V((4, RD, XD), f32), V((4, RD, XD), f32),
            V((4, 8, 128), f32), V((4, 8, 8, 128), f32), V((8, 128), f32), V((2, 128), f32), V((nd + 2, 2, 128), f32), V((nd + 2, 16, 8, 128), f32),
            V((nx, 16, 128), f32), V((2, 8, 128), f32), V((nd + 2, 8, 128), f32),
            V((nx, 4, 128), f32), V((nx, 4, 128), f32), V((4, 128), f32), V((4, 128), f32),
            V((nd + 2, 4, 128), f32), V((nd + 2, F, 2, 8, 8, 128), f32), V((3, F, 2, 8, 8, 128), f32),
            V((8, RD, XD), f32), V((6, RD, XD), f32),
            dma((12,)), dma((8,)), dma((8,)), dma((8,)), dma((8,)),
            dma, dma, dma, dma((nd,)), dma, dma, dma, dma, dma, dma((nd,)), dma, dma,
        ]
        return pl.pallas_call(
            functools.partial(kernel, nd, nx),
            out_shape=(V((2 * F, RD, XD), f32), V((2 * F, RD, XD), f32)),
            in_specs=[far] * 12,
            out_specs=(vmem, vmem),
            scratch_shapes=scratch,
            compiler_params=pltpu.CompilerParams(
                collective_id=0, has_side_effects=True, vmem_limit_bytes=60 << 20
            ),
        )(
            incident, inverse_diag, previous, heights, neighbours, counts, transmit, angle_weights,
            jnp.asarray(v_rows), jnp.asarray(u_rows), jnp.asarray(cell), jnp.asarray(wide),
        )

    placed = (
        P(None, "rng", "xr"),
        P(None, "rng", "xr"),
        P(None, "rng", "xr"),
        P("rng", "xr"),
        P(None, "rng", "xr"),
        P("rng", "xr"),
        P("rng", None, None),
        P(),
    )
    return jax.shard_map(
        per_device,
        mesh=mesh,
        in_specs=placed,
        out_specs=(P(None, "rng", "xr"), P(None, "rng", "xr")),
        check_vma=False,
    )
```

```python
import functools
import math

import jax
import jax.numpy as jnp
import numpy as np
from jax import lax
from jax.experimental import pallas as pl
from jax.experimental.pallas import tpu as pltpu
from jax.sharding import PartitionSpec as P

F = 2
Q = 64
H = 3
LMAX = 24
RD = 16
XD = 128
SIDE = 2 * H + 1
MESH = pl.DeviceIdType.MESH
f32 = jnp.float32
bf16 = jnp.bfloat16
i32 = jnp.int32


def phase_tables():
    turn = 2.0 * math.pi / 64
    power = np.arange(16) - 7
    cols = np.arange(XD)
    ang = turn * ((power[:, None] * cols[None, :]) % 64)
    v_rows = np.stack([np.cos(ang), np.sin(ang)]).astype(np.float32)
    u_rows = np.zeros((4, RD, 2, 16, XD), np.float32)
    cell = np.zeros((4, 12, RD, XD), np.float32)
    for dm in range(4):
        rows = 16 * dm + np.arange(RD)
        ang = turn * ((power[None, :] * rows[:, None]) % 64)
        u_rows[dm, :, 0] = np.cos(ang)[:, :, None]
        u_rows[dm, :, 1] = np.sin(ang)[:, :, None]
        for way, sign in enumerate((1, -1)):
            for f in range(F):
                ang = turn * ((sign * (1 + 2 * f) * rows[:, None] + (f - 4) * cols[None, :]) % 64)
                cell[dm, way * 4 + f * 2] = np.cos(ang)
                cell[dm, way * 4 + f * 2 + 1] = np.sin(ang)
        ang = turn * ((rows[:, None] + 0 * cols[None, :]) % 64)
        cell[dm, 8], cell[dm, 9] = np.cos(ang), np.sin(ang)
        ang = turn * ((0 * rows[:, None] + cols[None, :]) % 64)
        cell[dm, 10], cell[dm, 11] = np.cos(ang), np.sin(ang)
    lane = np.arange(XD)
    side = np.where(lane < 8, lane - 3, lane + 120)
    wide = np.zeros((4, 8, 4, RD, XD), np.float32)
    for dm in range(4):
        rows = 16 * dm - 8 + np.arange(32)
        row_at = np.stack([np.r_[rows[:8], rows[:8]], rows[8:24], rows[8:24], np.r_[rows[24:], rows[24:]]])
        half = np.concatenate([np.tile(lane, (8, 1)), np.tile(side, (8, 1))])
        col_at = np.stack([half, np.tile(lane, (RD, 1)), np.tile(side, (RD, 1)), half])
        row_at = row_at[:, :, None] + 0 * col_at
        angs = [(1 + 2 * f) * row_at + (f - 4) * col_at for f in range(F)] + [row_at, col_at]
        for n, ang in enumerate(angs):
            wide[dm, 2 * n] = np.cos(turn * (ang % 64))
            wide[dm, 2 * n + 1] = np.sin(turn * (ang % 64))
    return v_rows, u_rows, cell, wide


def sincos_small(t):
    q = t * t
    s = t * (1.0 + q * (-1.0 / 6 + q * (1.0 / 120 + q * (-1.0 / 5040 + q * (1.0 / 362880)))))
    c = 1.0 + q * (-0.5 + q * (1.0 / 24 + q * (-1.0 / 720 + q * (1.0 / 40320))))
    return s, c


def sincos(t):
    q = t * t
    s = t * (
        1.0
        + q
        * (
            -1.0 / 6
            + q * (1.0 / 120 + q * (-1.0 / 5040 + q * (1.0 / 362880 + q * (-1.0 / 39916800))))
        )
    )
    c = 1.0 + q * (
        -0.5
        + q
        * (
            1.0 / 24
            + q
            * (-1.0 / 720 + q * (1.0 / 40320 + q * (-1.0 / 3628800 + q * (1.0 / 479001600))))
        )
    )
    return s, c


def squared(c, s):
    return c * c - s * s, 2.0 * (c * s)


def lanes_of(shape):
    return lax.broadcasted_iota(i32, shape, 1)


def rows_of(shape):
    return lax.broadcasted_iota(i32, shape, 0)


def pick(value, index):
    return jnp.take_along_axis(value, index, axis=1, mode="promise_in_bounds")


def split(value):
    high = value.astype(bf16)
    return high, (value - high.astype(f32)).astype(bf16)


def contract(left, right):
    return lax.dot_general(left, right, (((1,), (1,)), ((), ())), preferred_element_type=f32)


def contract3(left_high, left_low, right_high, right_low):
    return (
        contract(left_high, right_high)
        + contract(left_high, right_low)
        + contract(left_low, right_high)
    )


def regroup(value):
    shape = (8, 128)
    part = (rows_of(shape) - lanes_of(shape) // 16) & 7
    out = jnp.zeros(shape, f32)
    for s in range(8):
        moved = value
        if s:
            moved = pltpu.roll(pltpu.roll(value, 128 - 16 * s, 1), s, 0)
        out = jnp.where(part == s, moved, out)
    return out


def kernel(
    nd, nx,
    inc_hbm, zin_hbm, prev_hbm, hts_hbm, nbr_hbm, cnt_hbm, trn_hbm, aw_hbm, v_hbm, u_hbm, cell_hbm, wide_hbm,
    out_f, out_c,
    inc, zin, prev, hts, nbr, cnt, trn, aw, v_rows, u_rows, cell, wide_cell, pz, psrc, pwave, cflow, eflow, near_rows, cbuf, edge_l, edge_r, pk_l, pk_r,
    cbuf2, edge_l2, edge_r2, pk_l2, pk_r2,
    shifted, table, tab_u_h, tab_u_l, tab_a_h, tab_a_l, tab_v, tab_f_h, tab_f_l,
    srcp, loaded, driven, weakf, w_lane, w_sub, row_buf, share_msg, tr, tb,
    gx, gmsg, gr, fx, fx2, fmsg, fmsg2, fr, mats, state,
    base, vu,
    csem, hs_sem, hr_sem, hs2_sem, hr2_sem,
    gxs, gxr, grs, grr, fxs, fxr, fxs2, fxr2, frs, frr, trs, trr,
):
    d = lax.axis_index("rng")
    x = lax.axis_index("xr")
    dm = lax.rem(d, 4)
    spread = 1.0 / math.sqrt(RD * XD * nx)
    up, down = lax.rem(d + nd - 1, nd), lax.rem(d + 1, nd)
    left, right = lax.rem(x + nx - 1, nx), lax.rem(x + 1, nx)

    def turned(value, by, size):
        moved = value + by
        return jnp.where(moved >= size, moved - size, moved)

    nc = min(4, nd)
    nr = nd // nc
    far = lambda n, size: min(n, size - n)
    others = sorted(
        ((a, b) for a in range(nr) for b in range(nc) if a or b),
        key=lambda p: -far(p[0], nr) - far(p[1], nc),
    )
    d_row, d_col = d // nc, lax.rem(d, nc)
    blocks = [turned(d_row, a, nr) * nc + turned(d_col, b, nc) for a, b in others]
    owners = [turned(x, n, nx) for n in sorted(range(1, nx), key=lambda n: -far(n, nx))]

    barrier = pltpu.get_barrier_semaphore()
    peers = [(to, x) for to in blocks] + [(d, to) for to in owners]
    peers += [(dd, xx) for dd in (up, down) for xx in (left, right)]
    for peer in peers:
        pl.semaphore_signal(barrier, inc=1, device_id=peer, device_id_type=MESH)

    fetches = [
        (prev_hbm, prev), (hts_hbm, hts), (zin_hbm, zin), (trn_hbm, trn), (v_hbm, v_rows), (u_hbm.at[dm], u_rows),
        (aw_hbm, aw), (cell_hbm.at[dm], cell), (cnt_hbm, cnt), (nbr_hbm, nbr), (inc_hbm, inc),
        (wide_hbm.at[dm], wide_cell),
    ]
    fetches = [pltpu.make_async_copy(a, b, csem.at[n]) for n, (a, b) in enumerate(fetches)]
    for fetch in fetches:
        fetch.start()

    wide = (RD, XD)
    lane16 = lanes_of(wide)
    small = (8, 128)
    lane8 = lanes_of(small)
    sub8 = rows_of(small)

    def pack_edges(parts, to_left, to_right):
        a = jnp.zeros(wide, f32)
        b = jnp.zeros(wide, f32)
        for c, part in enumerate(parts):
            here = lane16 // 8 == c
            a = jnp.where(here, part if c == 0 else pltpu.roll(part, 8 * c, 1), a)
            b = jnp.where(here, pltpu.roll(part, 8 * c + 3, 1), b)
        to_left[...] = a
        to_right[...] = b

    for fetch in fetches[:3]:
        fetch.wait()
    for c in range(4):
        cbuf[c, 8:24, :] = prev[c]
        cbuf[5 + c, 8:24, :] = zin[c]
    cbuf[4, 8:24, :] = hts[...]
    pack_edges([prev[c] for c in range(4)] + [hts[...]] + [zin[c] for c in range(4)], pk_l, pk_r)
    zero8 = jnp.zeros(small, f32)
    li, lj = lane8 // 16, lane8 % 16
    for slot in (0, nd + 1):
        gr[slot] = zero8
        fr[slot] = jnp.zeros((4, 128), f32)
        tr[slot] = jnp.zeros((2, 128), f32)
    fetches[3].wait()
    row_buf[...] = zero8
    row_buf[4:6, 0:Q] = trn[0]
    share_rows = jnp.where(lj < 8, pick(row_buf[...], (li * 8 + lj) & 127), 0.0)
    share_msg[...] = share_rows[4:6, :]
    tr[d + 1] = share_rows[4:6, :]

    def halo(buf, e_l, e_r, p_l, p_r, send, recv):
        plan = [
            (p_l.at[0:8, :], e_r.at[24:32, :], (up, left)),
            (p_l.at[8:16, :], e_r.at[0:8, :], (down, left)),
            (p_r.at[0:8, :], e_l.at[24:32, :], (up, right)),
            (p_r.at[8:16, :], e_l.at[0:8, :], (down, right)),
            (buf.at[:, 8:16, :], buf.at[:, 24:32, :], (up, x)),
            (buf.at[:, 16:24, :], buf.at[:, 0:8, :], (down, x)),
            (p_l, e_r.at[8:24, :], (d, left)),
            (p_r, e_l.at[8:24, :], (d, right)),
        ]
        return [
            pltpu.make_async_remote_copy(
                src_ref=src, dst_ref=dst, send_sem=send.at[n], recv_sem=recv.at[n],
                device_id=dev, device_id_type=MESH,
            )
            for n, (src, dst, dev) in enumerate(plan)
        ]

    for fetch in fetches[4:6]:
        fetch.wait()
    power16 = (rows_of(wide) - 7).astype(f32) * 0.03

    def fill(r, carry):
        at = pl.ds(pl.multiple_of(r * XD, XD), XD)
        hrow = jnp.broadcast_to(hts[pl.ds(r, 1), :], wide)
        hs, hc = sincos_small(power16 * hrow)
        vc0, vs0 = v_rows[0], v_rows[1]
        vc = hc * vc0 - hs * vs0
        vs = hc * vs0 + hs * vc0
        tab_v[0, :, at] = vc[:8]
        tab_v[1, :, at] = vs[:8]
        c8, s8 = squared(*squared(*squared(hc, hs)))
        pc, ps = u_rows[r, 0], u_rows[r, 1]
        cc_, ss_, cs_, sc_ = c8 * pc, s8 * ps, c8 * ps, s8 * pc
        for n, value in enumerate((cc_ - ss_, sc_ + cs_, cc_ + ss_, sc_ - cs_)):
            high, low = split(value)
            tab_u_h[16 * n : 16 * n + 16, at] = high
            tab_u_l[16 * n : 16 * n + 16, at] = low
        for f in range(F):
            zr = jnp.broadcast_to(zin[2 * f, pl.ds(r, 1), :], wide)
            zi = jnp.broadcast_to(zin[2 * f + 1, pl.ds(r, 1), :], wide)
            for n, value in enumerate((zr * vc - zi * vs, zr * vs + zi * vc)):
                high, low = split(value)
                k = 2 * f + n
                tab_a_h[16 * k : 16 * k + 16, at] = high
                tab_a_l[16 * k : 16 * k + 16, at] = low
        return carry

    lax.fori_loop(0, RD, fill, 0)

    y = contract3(tab_u_h[...], tab_u_l[...], tab_a_h[...], tab_a_l[...])
    yc = jnp.concatenate([y[0:16], y[32:48]], axis=1)
    ys = jnp.concatenate([y[16:32], y[48:64]], axis=1)
    gx[x] = yc + jnp.where((lane16 // 16) % 2 == 0, -pltpu.roll(ys, 112, 1), pltpu.roll(ys, 16, 1))

    def spread_xr(buf, send, recv):
        for to in owners:
            pltpu.make_async_remote_copy(
                src_ref=buf.at[x], dst_ref=buf.at[x], send_sem=send, recv_sem=recv,
                device_id=(d, to), device_id_type=MESH,
            ).start()

    def await_bytes(view, sem):
        pltpu.make_async_copy(view, view, sem).wait()

    def total_xr(buf):
        total = buf[0]
        for k in range(1, nx):
            total = total + buf[k]
        return total

    for fetch in fetches[6:]:
        fetch.wait()
    for f in range(F):
        for c in range(2):
            row_buf[2 * f + c : 2 * f + c + 1, 0:Q] = aw[f, c : c + 1, :]
    weight_rows = [jnp.broadcast_to(row_buf[k : k + 1, :], small) * spread for k in range(4)]
    for k in range(4):
        w_lane[k] = jnp.where(lj < 8, pick(weight_rows[k], (li * 8 + lj) & 127), 0.0)
    for i in range(8):
        for k in range(4):
            w_sub[k, i] = pick(weight_rows[k], sub8 + 8 * i)

    hh = hts[...]
    hs, hc = sincos_small(0.03 * hh)
    c8, s8 = squared(*squared(*squared(hc, hs)))
    vu[0] = hc * cell[10] - hs * cell[11]
    vu[1] = hc * cell[11] + hs * cell[10]
    vu[2] = c8 * cell[8] - s8 * cell[9]
    vu[3] = s8 * cell[8] + c8 * cell[9]
    vu[4] = c8 * cell[8] + s8 * cell[9]
    vu[5] = s8 * cell[8] - c8 * cell[9]
    for f in range(F):
        s, c = sincos((0.3 + 0.2 * f) * hh)
        for way in range(2):
            k = way * 4 + f * 2
            base[k] = c * cell[k] - s * cell[k + 1]
            base[k + 1] = s * cell[k] + c * cell[k + 1]

    def note(l, words):
        word0, word1 = words
        code = nbr[l]
        m = jnp.where(code >= 24, code + 1, code)
        low = m < 28
        bit = jnp.where(l < cnt[...], jnp.left_shift(1, jnp.where(low, m, m - 28)), 0)
        return word0 | jnp.where(low, bit, 0), word1 | jnp.where(low, 0, bit)

    zero_word = jnp.zeros(wide, i32)
    words = lax.fori_loop(0, LMAX, note, (zero_word, zero_word))

    pl.semaphore_wait(barrier, nd - 1 + nx - 1 + 4)
    halo1 = halo(cbuf, edge_l, edge_r, pk_l, pk_r, hs_sem, hr_sem)
    for copy in halo1:
        copy.start()
    spread_xr(gx, gxs, gxr)
    for to in blocks:
        pltpu.make_async_remote_copy(
            src_ref=share_msg, dst_ref=tr.at[d + 1], send_sem=trs, recv_sem=trr,
            device_id=(to, x), device_id_type=MESH,
        ).start()

    tall = (32, XD)
    lane32 = lanes_of(tall)
    row32 = rows_of(tall) + (d * RD - 8)
    inside = (row32 >= 0) & (row32 < nd * RD)

    def shift_all(buf, edges, count):
        to_left = inside & (lane32 < 128 * x)
        to_right = inside & (lane32 < 128 * (nx - 1 - x))
        for c in range(count):
            el, left_at, er, right_at = edges(c)
            el = jnp.where(to_left, el, 0.0)
            er = jnp.where(to_right, er, 0.0)
            mid = jnp.where(inside, buf[c], 0.0)
            shifted[H, c] = mid
            for k in range(1, H + 1):
                shifted[H + k, c] = jnp.where(
                    lane32 >= 128 - k,
                    pltpu.roll(er, (128 - k - right_at) % 128, 1),
                    pltpu.roll(mid, 128 - k, 1),
                )
                shifted[H - k, c] = jnp.where(
                    lane32 < k,
                    pltpu.roll(el, (k - 3 - left_at) % 128, 1),
                    pltpu.roll(mid, k, 1),
                )

    def sides(e_l, e_r, c):
        left_part = e_l[...] if c == 0 else pltpu.roll(e_l[...], 128 - 8 * c, 1)
        right_part = e_r[...] if c == 1 else pltpu.roll(e_r[...], (136 - 8 * c) % 128, 1)
        return jnp.where(lane32 < 8, left_part, right_part)

    def grouped(center, edge):
        return (
            jnp.concatenate([center[:8], edge[:8]], axis=0),
            center[8:24],
            edge[8:24],
            jnp.concatenate([center[24:], edge[24:]], axis=0),
        )

    def window(dyi, c, dx):
        return shifted[dyi, c, 8 + dx : 24 + dx, :]

    def applied(total, g, dyi, dx):
        out = []
        for f in range(F):
            gr_, gi_ = g[2 * f], g[2 * f + 1]
            ur, ui = window(dyi, 2 * f, dx), window(dyi, 2 * f + 1, dx)
            out.append(total[2 * f] + (gr_ * ur - gi_ * ui))
            out.append(total[2 * f + 1] + (gr_ * ui + gi_ * ur))
        return tuple(out)

    for copy in halo1:
        copy.wait_recv()
    shift_all(cbuf, lambda c: (edge_l[...], 8 * c, edge_r[...], 8 * c), 5)

    def couple(dyi, total):
        dy = dyi - H
        for dxi in range(SIDE):
            dx = dxi - H
            square = jnp.maximum(dx * dx + dy * dy, 1).astype(f32)
            rise = window(dyi, 4, dx) - hh
            dist2 = square + rise * rise
            inv = lax.rsqrt(dist2)
            inv = inv * (1.5 - 0.5 * dist2 * (inv * inv))
            bits = words[dxi // 4] >> (7 * (dxi % 4) + dyi)
            mag = jnp.where((bits & 1) == 1, 0.25 * inv, 0.0)
            s1, c1 = sincos((math.pi / 8) * (dist2 * inv) - 0.5 * math.pi)
            s1, c1 = c1, -s1
            c4, s4 = squared(*squared(c1, s1))
            g = (
                mag * c4,
                mag * s4,
                mag * (c4 * c1 - s4 * s1),
                mag * (s4 * c1 + c4 * s1),
            )
            for c in range(4):
                table[dyi, dxi, c] = g[c]
            total = applied(total, g, dyi, dx)
        return total

    def recouple(dyi, total):
        for dxi in range(SIDE):
            g = [table[dyi, dxi, c] for c in range(4)]
            total = applied(total, g, dyi, dxi - H)
        return total

    nothing = (jnp.zeros(wide, f32),) * 4
    near_old = lax.fori_loop(0, SIDE, couple, nothing)

    def times_z(f, real, imag):
        zr, zi = zin[2 * f], zin[2 * f + 1]
        return zr * real - zi * imag, zr * imag + zi * real

    def project(way, field, buf, send, recv):
        lj_even = (lane8 // 8) % 2 == 0
        for f in range(F):
            k = way * 4 + f * 2
            br, bi = base[k], base[k + 1]
            sr, si = field[2 * f], field[2 * f + 1]
            srcp[2 * f] = br * sr + bi * si
            srcp[2 * f + 1] = br * si - bi * sr

        def lay(r, carry):
            at = pl.ds(pl.multiple_of(r * XD, XD), XD)
            vc, vs = tab_v[0, :, at], tab_v[1, :, at]
            for f in range(F):
                sr = jnp.broadcast_to(srcp[2 * f, pl.ds(r, 1), :], small)
                si = jnp.broadcast_to(srcp[2 * f + 1, pl.ds(r, 1), :], small)
                both = jnp.concatenate([sr * vc - si * vs, sr * vs + si * vc], axis=0)
                high, low = split(both)
                tab_f_h[16 * f : 16 * f + 16, at] = high
                tab_f_l[16 * f : 16 * f + 16, at] = low
            return carry

        lax.fori_loop(0, RD, lay, 0)
        rows = slice(32 * way, 32 * way + 32)
        y = contract3(tab_u_h[rows, :], tab_u_l[rows, :], tab_f_h[...], tab_f_l[...])
        pad = jnp.zeros((8, 96), f32)
        yc = jnp.concatenate([y[0:8], pad], axis=1)
        ys = jnp.concatenate([y[16:24], pad], axis=1)
        sums = yc + jnp.where(lj_even, -pltpu.roll(ys, 120, 1), pltpu.roll(ys, 8, 1))
        for k in range(4):
            row = pick(sums, 8 * k + 7 - (lj & 7))
            row = jnp.where(sub8 == 7 - li, row, 0.0)
            buf[x, k : k + 1, :] = jnp.sum(row, axis=0, keepdims=True)
        spread_xr(buf, send, recv)

    for f in range(F):
        sr, si = times_z(f, inc[2 * f] - near_old[2 * f], inc[2 * f + 1] - near_old[2 * f + 1])
        loaded[2 * f] = sr
        loaded[2 * f + 1] = si
    project(0, loaded, fx, fxs, fxr)
    await_bytes(gx.at[pl.ds(0, nx - 1)], gxr)
    g_sum = total_xr(gx)
    h0, h1 = regroup(g_sum[:8]), regroup(g_sum[8:])
    gmsg[0] = jnp.where(sub8 < 4, h0, pltpu.roll(h1, 4, 0))
    gmsg[1] = jnp.where(sub8 < 4, pltpu.roll(h0, 4, 0), h1)

    for to in blocks:
        pltpu.make_async_remote_copy(
            src_ref=gmsg.at[(to < d).astype(i32)], dst_ref=gr.at[d + 1],
            send_sem=grs, recv_sem=grr.at[d],
            device_id=(to, x), device_id_type=MESH,
        ).start()

    gr[d + 1] = gmsg[0]

    for c in range(4):
        cbuf2[c, 8:24, :] = loaded[c]
    pack_edges([loaded[c] for c in range(4)], pk_l2, pk_r2)
    halo2 = halo(cbuf2, edge_l2, edge_r2, pk_l2, pk_r2, hs2_sem, hr2_sem)
    for copy in halo2:
        copy.start()

    for g, height in enumerate(grouped(cbuf[4], sides(edge_l, edge_r, 4))):
        hs, hc = sincos_small(0.03 * height)
        c8, s8 = squared(*squared(*squared(hc, hs)))
        pwave[4, g] = c8 * wide_cell[4, g] - s8 * wide_cell[5, g]
        pwave[5, g] = s8 * wide_cell[4, g] + c8 * wide_cell[5, g]
        pwave[6, g] = hc * wide_cell[6, g] - hs * wide_cell[7, g]
        pwave[7, g] = hc * wide_cell[7, g] + hs * wide_cell[6, g]
        for f in range(F):
            k = 2 * f
            s, c = sincos((0.3 + 0.2 * f) * height)
            pwave[k, g] = c * wide_cell[k, g] - s * wide_cell[k + 1, g]
            pwave[k + 1, g] = s * wide_cell[k, g] + c * wide_cell[k + 1, g]
    for c in range(4):
        for g, value in enumerate(grouped(cbuf[5 + c], sides(edge_l, edge_r, 5 + c))):
            pz[c, g] = value

    await_bytes(tr.at[pl.ds(0, nd - 1)], trr)

    def spread_shares(n, carry):
        for k in range(4):
            slot = 4 * n + (k + 1)
            index = (lane8 & 7) * 16 + sub8
            two = [pick(jnp.broadcast_to(tr[slot, f : f + 1, :], small), index) for f in range(F)]
            two = jnp.where(lane8 < 8, two[0], two[1])
            for at in range(16):
                tb[slot, at] = jnp.broadcast_to(two[:, at : at + 1], small)
        return carry

    lax.fori_loop(0, nd // 4, spread_shares, 0)

    def send_feed(way, buf, recv, msg):
        await_bytes(buf.at[pl.ds(0, nx - 1)], recv)
        msg[...] = total_xr(buf)
        if way == 0:
            fr[d + 1] = msg[...]
        for to in blocks:

            @pl.when(to < d if way else to > d)
            def _():
                pltpu.make_async_remote_copy(
                    src_ref=msg, dst_ref=fr.at[d + 1], send_sem=frs, recv_sem=frr.at[d],
                    device_id=(to, x), device_id_type=MESH,
                ).start()

    def await_slots(buf, sem, first, last):
        def step(k, carry):
            await_bytes(buf.at[k + 1], sem.at[k])
            return carry

        lax.fori_loop(first, last, step, 0)

    def build(slot, first):
        if first:
            start = (7 - li) * 16 + sub8 - lj + 7
        else:
            start = (li + 7) * 16 + lj - sub8 + 7
        g = [
            [jnp.broadcast_to(gr[slot, r : r + 1, :], small) for r in (k, 4 + k)]
            for k in range(4)
        ]
        for i in range(8):
            src = start + 16 * i if first else start - 16 * i
            index = src & 127
            near = src < 128
            m = [jnp.where(near, pick(g[k][0], index), pick(g[k][1], index)) for k in range(4)]
            own = lane8 == sub8 + 16 * i
            if not first:
                own = own | (lane8 == sub8 + (16 * i + 8))
            for f in range(F):
                mr, mi = m[2 * f], m[2 * f + 1]
                if first:
                    wr, wi = w_sub[2 * f, i], w_sub[2 * f + 1, i]
                else:
                    wr, wi = w_lane[2 * f], w_lane[2 * f + 1]
                real = jnp.where(own, 1.0, 0.0) - (mr * wr - mi * wi)
                imag = -(mr * wi + mi * wr)
                if not first:
                    share = tb[slot, 8 * f + i]
                    real, imag = share * real, share * imag
                mats[slot, f, 0, i] = real
                mats[slot, f, 1, i] = imag

    def slots_of(way, t):
        if way == 0:
            at = 2 * t - lax.rem(d, 2)
            return at + 1, at + 2
        at = 2 * t - lax.rem(nd - 1 - d, 2)
        return nd - at, nd - at - 1

    def pairs_of(way):
        return (d + 1) // 2 if way == 0 else (nd - d) // 2

    def await_blocks(way, buf, sem):
        if way == 0:
            await_slots(buf, sem, 0, d)
        else:
            await_slots(buf, sem, d + 1, nd)

    def build_all(way):
        def step(t, carry):
            one, two = slots_of(way, t)
            build(one, True)
            build(two, False)
            return carry

        lax.fori_loop(0, pairs_of(way), step, 0)

    def tree(terms):
        while len(terms) > 1:
            terms = [a + b for a, b in zip(terms[::2], terms[1::2])]
        return terms[0]

    def carry_rows(one, f):
        real, imag = [], []
        for i in range(8):
            mr, mi = mats[one, f, 0, i], mats[one, f, 1, i]
            sr, si = state[1, f, 0, i], state[1, f, 1, i]
            real.append(mr * sr - mi * si)
            imag.append(mr * si + mi * sr)
        share = tr[one, f : f + 1, :]
        return [
            share * (jnp.sum(tree(terms), axis=0, keepdims=True) + fr[one, 2 * f + c : 2 * f + c + 1, :])
            for c, terms in enumerate((real, imag))
        ]

    def sweep(way):
        for f in range(F):
            for c in range(2):
                for i in range(8):
                    state[1, f, c, i] = zero8

        def step(t, carry):
            one, two = slots_of(way, t)
            for f in range(F):
                y = []
                for c, row in enumerate(carry_rows(one, f)):
                    k = 2 * f + c
                    near_rows[k : k + 1, :] = row
                    row = row + jnp.where(lj[:1] < 8, 0.0, fr[two, k : k + 1, :])
                    y.append(jnp.broadcast_to(row, small))
                yr, yi = y
                for i in range(8):
                    mr, mi = mats[two, f, 0, i], mats[two, f, 1, i]
                    vr = jnp.sum(mr * yr - mi * yi, axis=1, keepdims=True)
                    vi = jnp.sum(mr * yi + mi * yr, axis=1, keepdims=True)
                    state[1, f, 0, i] = jnp.broadcast_to(vr, small)
                    state[1, f, 1, i] = jnp.broadcast_to(vi, small)
            return carry

        lax.fori_loop(0, pairs_of(way), step, 0)

    def neighbour_carries():
        before = [jnp.broadcast_to(near_rows[k : k + 1, :], small) for k in range(4)]
        after = []
        for f in range(F):
            after += [jnp.broadcast_to(row, small) for row in carry_rows(d + 1, f)]
        for i in range(8):
            index = sub8 + 16 * i
            for f in range(F):
                for c in range(2):
                    state[0, f, c, i] = pick(before[2 * f + c], index)
                    state[2, f, c, i] = pick(after[2 * f + c], index)

    def weigh(which):
        for f in range(F):
            for i in range(8):
                wr, wi = w_sub[2 * f, i], w_sub[2 * f + 1, i]
                sr, si = state[which, f, 0, i], state[which, f, 1, i]
                state[which, f, 0, i] = wr * sr - wi * si
                state[which, f, 1, i] = wr * si + wi * sr

    def radiate(which, v, u, bases):
        vr, vi = v
        ur, ui = u

        def step(n, total):
            i = 7 - n
            out = []
            for f in range(F):
                tr, ti = total[2 * f], total[2 * f + 1]

                def coef(c, j):
                    return jnp.broadcast_to(state[which, f, c, i, j : j + 1, :], wide)

                ar, ai = coef(0, 7), coef(1, 7)
                for j in range(6, -1, -1):
                    ar, ai = ar * vr - ai * vi + coef(0, j), ar * vi + ai * vr + coef(1, j)
                out += [tr * ur - ti * ui + ar, tr * ui + ti * ur + ai]
            return tuple(out)

        total = lax.fori_loop(0, 8, step, nothing)
        out = []
        for f in range(F):
            br, bi = bases[2 * f], bases[2 * f + 1]
            tr, ti = total[2 * f], total[2 * f + 1]
            out += [br * tr - bi * ti, br * ti + bi * tr]
        return out

    send_feed(0, fx, fxr, fmsg)
    await_blocks(0, gr, grr)
    build_all(0)
    build(d + 1, True)
    near_rows[...] = jnp.zeros((4, 128), f32)
    for copy in halo2:
        copy.wait_recv()
    for c in range(4):
        for g, value in enumerate(grouped(cbuf2[c], sides(edge_l2, edge_r2, c))):
            psrc[c, g] = value
    await_blocks(0, fr, frr)
    sweep(0)
    neighbour_carries()
    for which in range(3):
        weigh(which)
    for g in range(4):
        weak = radiate(
            (g + 1) // 2, (pwave[6, g], pwave[7, g]), (pwave[4, g], pwave[5, g]), [pwave[k, g] for k in range(4)]
        )
        for f in range(F):
            zr, zi = pz[2 * f, g], pz[2 * f + 1, g]
            wr, wi = weak[2 * f], weak[2 * f + 1]
            for c, flow in (
                (2 * f, psrc[2 * f, g] - (zr * wr - zi * wi)),
                (2 * f + 1, psrc[2 * f + 1, g] - (zr * wi + zi * wr)),
            ):
                if g == 1:
                    out_f[c] = flow
                    weakf[c] = weak[c]
                    cflow[c, 8:24, :] = flow
                elif g == 2:
                    eflow[c, 8:24, :] = flow
                else:
                    at = slice(0, 8) if g == 0 else slice(24, 32)
                    cflow[c, at, :] = flow[:8]
                    eflow[c, at, :] = flow[8:]
    shift_all(cflow, lambda c: (eflow[c], 0, eflow[c], 8), 4)
    near_new = lax.fori_loop(0, SIDE, recouple, nothing)
    for f in range(F):
        dr, di = times_z(
            f,
            inc[2 * f] - near_new[2 * f] - weakf[2 * f],
            inc[2 * f + 1] - near_new[2 * f + 1] - weakf[2 * f + 1],
        )
        driven[2 * f] = dr
        driven[2 * f + 1] = di
    project(1, driven, fx2, fxs2, fxr2)
    await_blocks(1, gr, grr)
    build_all(1)
    send_feed(1, fx2, fxr2, fmsg2)
    await_blocks(1, fr, frr)
    sweep(1)
    weigh(1)
    weak = radiate(1, (vu[0], vu[1]), (vu[4], vu[5]), [base[4 + k] for k in range(4)])
    for f in range(F):
        ar, ai = times_z(f, weak[2 * f], weak[2 * f + 1])
        out_c[2 * f] = driven[2 * f] - ar
        out_c[2 * f + 1] = driven[2 * f + 1] - ai

    for copy in halo1 + halo2:
        copy.wait_send()
    await_bytes(gx.at[pl.ds(0, nx - 1)], gxs)
    await_bytes(fx.at[pl.ds(0, nx - 1)], fxs)
    await_bytes(fx2.at[pl.ds(0, nx - 1)], fxs2)
    await_bytes(gr.at[pl.ds(0, nd - 1)], grs)
    await_bytes(fr.at[pl.ds(0, nd - 1)], frs)
    await_bytes(tr.at[pl.ds(0, nd - 1)], trs)


def solution(mesh):
    nd, nx = mesh.shape["rng"], mesh.shape["xr"]
    v_rows, u_rows, cell, wide = phase_tables()

    def per_device(incident, inverse_diag, previous, heights, neighbours, counts, transmit, angle_weights):
        vmem = pl.BlockSpec(memory_space=pltpu.VMEM)
        far = pl.BlockSpec(memory_space=pltpu.HBM)
        points = RD * XD
        V = pltpu.VMEM
        dma = pltpu.SemaphoreType.DMA
        held = [V(a.shape, a.dtype) for a in (
            incident, inverse_diag, previous, heights, neighbours, counts, transmit, angle_weights, v_rows
        )]
        scratch = held + [
            V((RD, 2, 16, XD), f32), V((12, RD, XD), f32),
            V((8, 4, RD, XD), f32), V((4, 4, RD, XD), f32), V((4, 4, RD, XD), f32), V((8, 4, RD, XD), f32),
            V((4, 32, XD), f32), V((4, 32, XD), f32), V((4, 128), f32),
            V((9, 32, XD), f32), V((32, XD), f32), V((32, XD), f32), V((RD, XD), f32), V((RD, XD), f32),
            V((4, 32, XD), f32), V((32, XD), f32), V((32, XD), f32), V((RD, XD), f32), V((RD, XD), f32),
            V((SIDE, 5, 32, XD), f32), V((SIDE, SIDE, 4, RD, XD), f32),
            V((64, points), bf16), V((64, points), bf16), V((64, points), bf16), V((64, points), bf16),
            V((2, 8, points), f32), V((32, points), bf16), V((32, points), bf16),
            V((4, RD, XD), f32), V((4, RD, XD), f32), V((4, RD, XD), f32), V((4, RD, XD), f32),
            V((4, 8, 128), f32), V((4, 8, 8, 128), f32), V((8, 128), f32), V((2, 128), f32), V((nd + 2, 2, 128), f32), V((nd + 2, 16, 8, 128), f32),
            V((nx, 16, 128), f32), V((2, 8, 128), f32), V((nd + 2, 8, 128), f32),
            V((nx, 4, 128), f32), V((nx, 4, 128), f32), V((4, 128), f32), V((4, 128), f32),
            V((nd + 2, 4, 128), f32), V((nd + 2, F, 2, 8, 8, 128), f32), V((3, F, 2, 8, 8, 128), f32),
            V((8, RD, XD), f32), V((6, RD, XD), f32),
            dma((12,)), dma((8,)), dma((8,)), dma((8,)), dma((8,)),
            dma, dma, dma, dma((nd,)), dma, dma, dma, dma, dma, dma((nd,)), dma, dma,
        ]
        return pl.pallas_call(
            functools.partial(kernel, nd, nx),
            out_shape=(V((2 * F, RD, XD), f32), V((2 * F, RD, XD), f32)),
            in_specs=[far] * 12,
            out_specs=(vmem, vmem),
            scratch_shapes=scratch,
            compiler_params=pltpu.CompilerParams(
                collective_id=0, has_side_effects=True, vmem_limit_bytes=60 << 20
            ),
        )(
            incident, inverse_diag, previous, heights, neighbours, counts, transmit, angle_weights,
            jnp.asarray(v_rows), jnp.asarray(u_rows), jnp.asarray(cell), jnp.asarray(wide),
        )

    placed = (
        P(None, "rng", "xr"),
        P(None, "rng", "xr"),
        P(None, "rng", "xr"),
        P("rng", "xr"),
        P(None, "rng", "xr"),
        P("rng", "xr"),
        P("rng", None, None),
        P(),
    )
    return jax.shard_map(
        per_device,
        mesh=mesh,
        in_specs=placed,
        out_specs=(P(None, "rng", "xr"), P(None, "rng", "xr")),
        check_vma=False,
    )
```
